128 devices in a mesh: seq: 64 (over y_hi, z, x, core), dp: 2 (over y_lo).
Axes of the slice: x: 4, y: 4 (y_hi: 2, y_lo: 2; y = y_hi * 2 + y_lo), z: 4, core: 2. Of those that a mesh axis runs over, the one named last changes fastest.
Arguments:
- inputs: bfloat16 [2, 32768, 4096], P('dp', 'seq'), may hold values from -60 to 60
- cotangent: bfloat16 [2, 32768, 4096], P('dp', 'seq'), may hold values from -16 to 16
- w_qkv: bfloat16 [4096, 768], replicated, may hold values from -0.09375 to 0.09375
- w_out: bfloat16 [512, 4096], replicated, may hold values from -0.25 to 0.25
- doc_start: int32 [2, 32768], P('dp', 'seq'), may hold values from 0 to 31744, as said below
Outputs:
- input_grad: bfloat16 [2, 32768, 4096], P('dp', 'seq')
- qkv_grad: float32 [4096, 768], P(('seq', 'dp'))
- out_grad: float32 [512, 4096], P(None, ('seq', 'dp'))
The draws below stay inside these ranges and needn't reach their ends.
Inputs may be any that keep to these rules, and one draw needn't show every extreme that they name: doc_start[b, p] is the first position of the document holding position p of row b; documents are contiguous runs. Cut a row into blocks of 512 positions: a document lies inside one block and then begins at a multiple of 64, or it fills exactly w whole blocks, w a power of two from 2 to 4, beginning at block 0 or at a block whose index minus 4/2 is a multiple of w. The first 2 blocks of a row form one document, and so do the last 2 blocks; the two blocks at the middle of a row lie in one document of 4 blocks.
All inputs are finite; a program needn't handle non-finite values.
Results may differ from the reference program's by a relative error of at most 0.025.
The reference program's roundings to bfloat16 on the way (of `attended_grad`, `rounded`, `attended`, `score_grad` and `merged_grad`) count: a program that leaves them out, or rounds other values in their place, can miss the bound.
Values may be sent and summed in bfloat16 or wider, within the bound.
A program may use at most 128 MiB of HBM per device.

```python
import jax
import jax.numpy as jnp
from jax import lax

D = 4096
HEAD = 128
HEADS = 4
SPAN = 4
TOK_DEV = 512
SEQLEN = 32768
BATCH = 2


def draw_doc_start(key, part):
    dev_count = SEQLEN // TOK_DEV
    half_span = SPAN // 2
    groups = (dev_count - SPAN) // SPAN
    levels = SPAN.bit_length()
    key_level, key_cut = jax.random.split(key, 2)
    group_level = jax.random.randint(key_level, (BATCH, groups), 0, levels)
    group_index = jnp.arange(groups, dtype=jnp.int32)[None, :]
    middle_group = (dev_count // 2 - half_span) // SPAN
    group_level = jnp.where(group_index == middle_group, 0, group_level)
    group_width = SPAN // jnp.left_shift(1, group_level)
    device = jnp.arange(dev_count, dtype=jnp.int32)
    inner = jnp.clip(device - half_span, 0, groups * SPAN - 1)
    group_of = inner // SPAN
    width_mid = group_width[:, group_of]
    first_mid = half_span + group_of[None, :] * SPAN + (inner[None, :] - group_of[None, :] * SPAN) // width_mid * width_mid
    device_row = device[None, :]
    tail = device_row >= dev_count - half_span
    head_part = device_row < half_span
    width_dev = jnp.where(head_part, half_span, jnp.where(tail, half_span, width_mid))
    group_first = jnp.where(head_part, 0, jnp.where(tail, dev_count - half_span, first_mid))
    piece_len = TOK_DEV // 8
    cut_bits = jax.random.randint(key_cut, (BATCH, dev_count, 8), 0, 2)
    cut_bits = cut_bits.at[:, :, 0].set(1)
    cut_bits = cut_bits.at[:, :, 7].set(1)
    cut_marks = jnp.arange(8, dtype=jnp.int32)[None, None, :] * cut_bits
    last_cut = lax.cummax(cut_marks, axis=2)
    local_piece = jnp.arange(TOK_DEV, dtype=jnp.int32) // piece_len
    within = last_cut[:, :, local_piece] * piece_len
    long_start = (group_first * TOK_DEV)[:, :, None]
    short_start = (device_row * TOK_DEV)[:, :, None] + within
    starts = jnp.where((width_dev > 1)[:, :, None], long_start, short_start)
    return starts.reshape(BATCH, SEQLEN).astype(jnp.int32)


def draw_inputs(key, part):
    key_main = jax.random.fold_in(key, 0)
    values = jnp.clip(jax.random.normal(key_main, (BATCH, SEQLEN, D), jnp.float32), -6.0, 6.0)
    return values.astype(jnp.bfloat16)


def spiked(values, rng, source, target, parts, factor):
    def block_of(axis_at):
        return (jnp.arange(values.shape[axis_at]) // (values.shape[axis_at] // parts)).reshape((-1,) + (1,) * (values.ndim - 1 - axis_at))

    first = jax.random.permutation(rng, parts)[block_of(target)]
    other_side = (block_of(target) + parts // 2) % parts
    return jnp.where((block_of(source) == first) | (block_of(source) == other_side), factor * values, values)


def steps_of(stream_key, dims, cuts, smallest, high):
    def one(axis_at, blocks):
        draws = jax.random.uniform(jax.random.fold_in(jax.random.fold_in(stream_key, 6), axis_at), (blocks,), jnp.float32, smallest / len(cuts), high / len(cuts))
        return jnp.repeat(jnp.exp(draws), dims[axis_at] // blocks).reshape((-1,) + (1,) * (len(dims) - axis_at - 1))

    level = one(*cuts[0])
    for cut in cuts[1:]:
        level = level * one(*cut)
    return level


def centred(key, dims, spread, limit, cuts=(), kind=jnp.bfloat16):
    array = spread * jax.random.normal(key, dims, jnp.float32)
    if cuts:
        array = array * steps_of(key, dims, cuts, -0.22, 0.18)
    return jnp.clip(array, -limit, limit).astype(kind)


def heavy_noise(key, extent, spread, limit, cuts, heavy, kind=jnp.bfloat16):
    entries = spread * jax.random.normal(key, extent, jnp.float32)
    if cuts:
        entries = entries * steps_of(key, extent, cuts, -0.22, 0.18)
    return jnp.clip(spiked(entries, jax.random.fold_in(key, 3), *heavy), -limit, limit).astype(kind)


def setup_inputs(seed: int = 0) -> dict:
    streams_of = jax.random.split(jax.random.key(seed), 6)
    inputs = draw_inputs(jax.random.fold_in(streams_of[5], 71), 0)
    cotangent = heavy_noise(streams_of[1], (BATCH, SEQLEN, D), 1.0, 16.0, ((0, 2), (1, 64)), (1, 2, 64, 4.0))
    w_qkv = centred(streams_of[2], (D, HEADS * HEAD + 2 * HEAD), D ** -0.5, 0.09375)
    w_out = centred(streams_of[3], (HEADS * HEAD, D), (HEADS * HEAD) ** -0.5, 0.25)
    doc_start = draw_doc_start(jax.random.fold_in(streams_of[5], 71), 0)
    return {"inputs": inputs, "cotangent": cotangent, "w_qkv": w_qkv, "w_out": w_out, "doc_start": doc_start}


rope_theta = 500000.0


def rope_tables(offsets):
    half_width = HEAD // 2
    frequency = rope_theta ** (-2.0 * jnp.arange(half_width, dtype=jnp.float32) / HEAD)
    angles = offsets.astype(jnp.float32)[:, None] * frequency[None, :]
    angles = jnp.concatenate([angles, angles], axis=1)
    return jnp.cos(angles), jnp.sin(angles)


def rotate(vector, cosine_table, sine_table):
    half_width = vector.shape[-1] // 2
    rotated = jnp.concatenate([-vector[..., half_width:], vector[..., :half_width]], axis=-1)
    return vector * cosine_table + rotated * sine_table


def rotate_back(gradient, cosine_table, sine_table):
    half_width = gradient.shape[-1] // 2
    weighted = gradient * sine_table
    return gradient * cosine_table + jnp.concatenate([weighted[..., half_width:], -weighted[..., :half_width]], axis=-1)


def hold_value(value_in):
    return lax.optimization_barrier(value_in)


def one_row(tokens, upstream, doc_row, w_qkv, w_out):
    seq_len = tokens.shape[0]
    query_width = HEADS * HEAD
    scaling = HEAD ** -0.5
    positions = jnp.arange(seq_len, dtype=jnp.int32)
    cosine_table, sine_table = rope_tables(positions - doc_row)
    projected = jnp.dot(tokens, w_qkv, preferred_element_type=jnp.float32)
    queries = hold_value(rotate(projected[:, :query_width].reshape(seq_len, HEADS, HEAD), cosine_table[:, None, :], sine_table[:, None, :]).astype(jnp.bfloat16))
    keys_all = hold_value(rotate(projected[:, query_width:query_width + HEAD], cosine_table, sine_table).astype(jnp.bfloat16))
    values_all = hold_value(projected[:, query_width + HEAD:].astype(jnp.bfloat16))
    attended_grad = hold_value(jnp.dot(upstream, w_out.T, preferred_element_type=jnp.float32).astype(jnp.bfloat16)).reshape(seq_len, HEADS, HEAD)
    margin = (SPAN - 1) * TOK_DEV
    window = SPAN * TOK_DEV
    padded = jnp.concatenate([jnp.zeros((margin, 2 * HEAD), jnp.bfloat16), jnp.concatenate([keys_all, values_all], axis=1)], axis=0)
    block_count = seq_len // TOK_DEV

    def block_step(kv_grads, block_index):
        row_first = (block_index * TOK_DEV).astype(jnp.int32)
        query_block = lax.dynamic_slice_in_dim(queries, row_first, TOK_DEV, 0).astype(jnp.float32)
        grad_block = lax.dynamic_slice_in_dim(attended_grad, row_first, TOK_DEV, 0).astype(jnp.float32)
        start_block = lax.dynamic_slice_in_dim(doc_row, row_first, TOK_DEV, 0)
        kv_window = lax.dynamic_slice_in_dim(padded, row_first, window, 0).astype(jnp.float32)
        key_pos = row_first - margin + jnp.arange(window, dtype=jnp.int32)
        query_pos = row_first + jnp.arange(TOK_DEV, dtype=jnp.int32)
        allowed = (key_pos[None, :] >= start_block[:, None]) & (key_pos[None, :] <= query_pos[:, None])
        scores = jnp.einsum("phe,te->hpt", query_block, kv_window[:, :HEAD]) * scaling
        row_max = jnp.max(jnp.where(allowed[None], scores, -jnp.inf), axis=2)
        row_total = jnp.sum(jnp.where(allowed[None], jnp.exp(scores - row_max[:, :, None]), 0.0), axis=2)
        log_total = row_max + jnp.log(row_total)
        probability = jnp.where(allowed[None], jnp.exp(scores - log_total[:, :, None]), 0.0)
        rounded = hold_value(probability.astype(jnp.bfloat16)).astype(jnp.float32)
        attended = hold_value(jnp.einsum("hpt,te->phe", rounded, kv_window[:, HEAD:]).astype(jnp.bfloat16)).astype(jnp.float32)
        row_delta = jnp.einsum("phe,phe->hp", grad_block, attended)
        prob_grad = jnp.einsum("phe,te->hpt", grad_block, kv_window[:, HEAD:])
        score_grad = hold_value((probability * (prob_grad - row_delta[:, :, None])).astype(jnp.bfloat16)).astype(jnp.float32)
        query_grad = jnp.einsum("hpt,te->phe", score_grad, kv_window[:, :HEAD]) * scaling
        key_grad = jnp.einsum("hpt,phe->te", score_grad, query_block) * scaling
        value_grad = jnp.einsum("hpt,phe->te", rounded, grad_block)
        current = lax.dynamic_slice_in_dim(kv_grads, row_first, window, 0)
        kv_grads = lax.dynamic_update_slice_in_dim(kv_grads, current + jnp.concatenate([key_grad, value_grad], axis=1), row_first, 0)
        return kv_grads, (attended, query_grad)

    kv_grads, (attended, query_grad) = lax.scan(block_step, jnp.zeros((seq_len + margin, 2 * HEAD), jnp.float32), jnp.arange(block_count, dtype=jnp.int32))
    kv_grads = kv_grads[margin:]
    query_pre = rotate_back(query_grad.reshape(seq_len, HEADS, HEAD), cosine_table[:, None, :], sine_table[:, None, :]).reshape(seq_len, query_width)
    key_pre = rotate_back(kv_grads[:, :HEAD], cosine_table, sine_table)
    merged_grad = hold_value(jnp.concatenate([query_pre, key_pre, kv_grads[:, HEAD:]], axis=1).astype(jnp.bfloat16))
    input_grad = jnp.dot(merged_grad, w_qkv.T, preferred_element_type=jnp.float32).astype(jnp.bfloat16)
    qkv_part = jnp.dot(tokens.T, merged_grad, preferred_element_type=jnp.float32)
    flat_attended = attended.reshape(seq_len, query_width).astype(jnp.bfloat16)
    out_part = jnp.dot(flat_attended.T, upstream, preferred_element_type=jnp.float32)
    return input_grad, qkv_part, out_part


def reference(inputs, cotangent, w_qkv, w_out, doc_start):
    results = [one_row(inputs[row_index], cotangent[row_index], doc_start[row_index], w_qkv, w_out) for row_index in range(BATCH)]
    input_grad = jnp.stack([result[0] for result in results], axis=0)
    qkv_grad = results[0][1]
    out_grad = results[0][2]
    for result in results[1:]:
        qkv_grad = qkv_grad + result[1]
        out_grad = out_grad + result[2]
    return input_grad, qkv_grad, out_grad
```

```python
from functools import partial

import jax
import jax.numpy as jnp
from jax import lax
from jax.experimental import pallas as pl
from jax.experimental.pallas import tpu as pltpu
from jax.sharding import PartitionSpec as P

HEAD = 128
HEADS = 4
SPAN = 4


rope_theta = 500000.0


def from_behind(block, axis, distance):
    devices = range(lax.axis_size(axis))
    route = [(i - distance, i) for i in devices if i - distance in devices]
    return lax.ppermute(block, axis, route)


def rope_tables(offsets):
    half_width = HEAD // 2
    frequency = rope_theta ** (-2.0 * jnp.arange(half_width, dtype=jnp.float32) / HEAD)
    angles = offsets.astype(jnp.float32)[:, None] * frequency[None, :]
    angles = jnp.concatenate([angles, angles], axis=1)
    return (jnp.cos(angles), jnp.sin(angles))


def rotate(vector, cosine_table, sine_table):
    half_width = vector.shape[-1] // 2
    rotated = jnp.concatenate([-vector[..., half_width:], vector[..., :half_width]], axis=-1)
    return vector * cosine_table + rotated * sine_table


def rotate_back(gradient, cosine_table, sine_table):
    half_width = gradient.shape[-1] // 2
    weighted = gradient * sine_table
    return gradient * cosine_table + jnp.concatenate(
        [weighted[..., half_width:], -weighted[..., :half_width]], axis=-1
    )


AXES = 4
ROWS = 32
LANES = 128
STREAMS = 10
BF16 = jnp.bfloat16
F32 = jnp.float32
MESH_ID = pl.DeviceIdType.MESH


def even_pair(i):
    return i + 1 - 2 * (i % 2)


def odd_pair(i):
    return (i + 3 - 2 * (i % 2)) % AXES


def stream_plan(g):
    order = ((0, 1, 2), (1, 2, 0), (2, 0, 1))[g % 3]
    first, second = (even_pair, odd_pair) if (g // 3) % 2 == 0 else (odd_pair, even_pair)
    return order, first, second


def device_of(x, y, z, core):
    return ((((y // 2) * AXES + z) * AXES + x) * 2 + core, y % 2)


def reduce_kernel(q_ref, o_ref, q_out, o_out, q_in, o_in, held, r1a, r1b, r2a, r2b, r3a, r3b, sib_sem, send_sem, recv_sem):
    seq = lax.axis_index("seq")
    dp = lax.axis_index("dp")
    core = seq % 2
    here = ((seq // 2) % AXES, (seq // 32) * 2 + dp, (seq // 8) % AXES)
    sibling = device_of(here[0], here[1], here[2], 1 - core)

    def moved(axis, value):
        spot = list(here)
        spot[axis] = value
        return device_of(*spot, core)

    barrier = pltpu.get_barrier_semaphore()
    pl.semaphore_signal(barrier, inc=1, device_id=sibling, device_id_type=MESH_ID)
    for axis in range(3):
        for pair in (even_pair, odd_pair):
            pl.semaphore_signal(barrier, inc=1, device_id=moved(axis, pair(here[axis])), device_id_type=MESH_ID)
    pl.semaphore_wait(barrier, 7)

    swaps = []
    for n, (src, dst) in enumerate(((q_ref, q_in), (o_ref, o_in))):
        swap = pltpu.make_async_remote_copy(
            src_ref=src.at[:, 1 - core],
            dst_ref=dst,
            send_sem=sib_sem.at[0, n],
            recv_sem=sib_sem.at[1, n],
            device_id=sibling,
            device_id_type=MESH_ID,
        )
        swap.start()
        swaps.append(swap)
    for swap in swaps:
        swap.wait_recv()

    def combine(block, _):
        y_hi = block // 16
        z = (block // 4) % 4
        x = block % 4
        for y_lo in range(2):
            spot = (x, y_hi * 2 + y_lo, z)
            rows = slice(y_lo * ROWS, (y_lo + 1) * ROWS)
            for g in range(STREAMS):
                order, _, _ = stream_plan(g)
                place = (spot[order[0]] * AXES + spot[order[1]]) * AXES + spot[order[2]]
                src, got, col = (q_ref, q_in, g) if g < 6 else (o_ref, o_in, g - 6)
                cols = slice(col * LANES, (col + 1) * LANES)
                total = src[block, core, rows, cols].astype(F32) + got[block, rows, cols].astype(F32)
                held[g, place] = total.astype(BF16)
        return 0

    lax.fori_loop(0, 32, combine, 0)

    def copy(src, dst, g, n, target):
        return pltpu.make_async_remote_copy(
            src_ref=src,
            dst_ref=dst,
            send_sem=send_sem.at[g, n],
            recv_sem=recv_sem.at[g, n],
            device_id=target,
            device_id_type=MESH_ID,
        )

    def add_into(dst, dst_at, src, src_at, count):
        def step(k, _):
            dst[dst_at + (k,)] = (dst[dst_at + (k,)].astype(F32) + src[src_at(k)].astype(F32)).astype(BF16)
            return 0

        if count == 1:
            step(0, 0)
        else:
            lax.fori_loop(0, count, step, 0)

    bufs = ((r1a, r1b), (r2a, r2b), (r3a, r3b))
    sizes = (16, 4, 1)
    sends = {}

    def source(g, stage):
        if stage == 0:
            return held, g
        return bufs[stage - 1][1], g

    def start_first(g, stage):
        order, first, second = stream_plan(g)
        i = here[order[stage]]
        size = sizes[stage]
        f = first(i)
        src, _ = source(g, stage)
        for slot, index in ((1, second(f)), (0, f)):
            sends[g, stage, slot] = copy(
                src.at[g, pl.ds(index * size, size)],
                bufs[stage][0].at[g, slot],
                g,
                stage * 3 + slot,
                moved(order[stage], f),
            )
            sends[g, stage, slot].start()

    for g in range(STREAMS):
        start_first(g, 0)
    for stage in range(3):
        size = sizes[stage]
        for g in range(STREAMS):
            order, first, second = stream_plan(g)
            i = here[order[stage]]
            s = second(i)
            src, _ = source(g, stage)
            sends[g, stage, 1].wait_recv()
            add_into(bufs[stage][0], (g, 1), src, lambda k, s=s, g=g: (g, s * size + k), size)
            sends[g, stage, 2] = copy(bufs[stage][0].at[g, 1], bufs[stage][1].at[g], g, stage * 3 + 2, moved(order[stage], s))
            sends[g, stage, 2].start()
            sends[g, stage, 0].wait_recv()
            add_into(bufs[stage][0], (g, 0), src, lambda k, i=i, g=g: (g, i * size + k), size)
        for g in range(STREAMS):
            sends[g, stage, 2].wait_recv()
            if stage < 2:
                add_into(bufs[stage][1], (g,), bufs[stage][0], lambda k, g=g: (g, 0, k), size)
                start_first(g, stage + 1)
            else:
                total = r3b[g, 0].astype(F32) + r3a[g, 0, 0].astype(F32)
                if g < 6:
                    q_out[:, g * LANES : (g + 1) * LANES] = total
                else:
                    o_out[:, (g - 6) * LANES : (g - 5) * LANES] = total
    for swap in swaps:
        swap.wait_send()
    for send in sends.values():
        send.wait_send()


def reduce_terms(q_term, o_term):
    vmem = pl.BlockSpec(memory_space=pltpu.VMEM)
    tile = (ROWS, LANES)
    return pl.pallas_call(
        reduce_kernel,
        out_shape=(
            jax.ShapeDtypeStruct((ROWS, 768), F32),
            jax.ShapeDtypeStruct((ROWS, 512), F32),
        ),
        in_specs=[vmem, vmem],
        out_specs=(vmem, vmem),
        scratch_shapes=[
            pltpu.VMEM((32, 2 * ROWS, 768), BF16),
            pltpu.VMEM((32, 2 * ROWS, 512), BF16),
            pltpu.VMEM((STREAMS, 64) + tile, BF16),
            pltpu.VMEM((STREAMS, 2, 16) + tile, BF16),
            pltpu.VMEM((STREAMS, 16) + tile, BF16),
            pltpu.VMEM((STREAMS, 2, 4) + tile, BF16),
            pltpu.VMEM((STREAMS, 4) + tile, BF16),
            pltpu.VMEM((STREAMS, 2, 1) + tile, BF16),
            pltpu.VMEM((STREAMS, 1) + tile, BF16),
            pltpu.SemaphoreType.DMA((2, 2)),
            pltpu.SemaphoreType.DMA((STREAMS, 9)),
            pltpu.SemaphoreType.DMA((STREAMS, 9)),
        ],
        compiler_params=pltpu.CompilerParams(
            collective_id=0, has_side_effects=True, vmem_limit_bytes=60 * 1024 * 1024
        ),
    )(q_term.reshape(32, 2, 2 * ROWS, 768), o_term.reshape(32, 2, 2 * ROWS, 512))


def per_device(inputs, cotangent, w_qkv, w_out, doc_start):
    tokens = inputs[0]
    upstream = cotangent[0]
    query_start = doc_start[0]
    rows_here = tokens.shape[0]
    scaling = HEAD ** (-0.5)
    query_width = HEADS * HEAD
    device_index = lax.axis_index("seq")
    query_pos = device_index * rows_here + jnp.arange(rows_here, dtype=jnp.int32)
    cosine_table, sine_table = rope_tables(query_pos - query_start)
    projected = jnp.dot(tokens, w_qkv, preferred_element_type=jnp.float32)
    queries = rotate(
        projected[:, :query_width].reshape(rows_here, HEADS, HEAD),
        cosine_table[:, None, :],
        sine_table[:, None, :],
    ).astype(jnp.bfloat16)
    rotated_keys = rotate(projected[:, query_width : query_width + HEAD], cosine_table, sine_table)
    key_value = jnp.concatenate([rotated_keys, projected[:, query_width + HEAD :]], axis=1).astype(
        jnp.bfloat16
    )
    attended_grad = (
        lax.dot_general(
            upstream, w_out, (((1,), (1,)), ((), ())), preferred_element_type=jnp.float32
        )
        .astype(jnp.bfloat16)
        .reshape(rows_here, HEADS, HEAD)
    )
    received = [key_value]
    travelling = key_value
    for offset in range(1, SPAN):
        travelling = from_behind(travelling, "seq", 1)
        received.append(travelling)
    key_firsts = [(device_index - offset) * rows_here for offset in range(SPAN)]
    active_list = [query_start[0] <= key_firsts[offset] + rows_here - 1 for offset in range(SPAN)]

    def tile_scores(kv_block, key_first):
        key_pos = key_first + jnp.arange(kv_block.shape[0], dtype=jnp.int32)
        allowed = (key_pos[None, :] >= query_start[:, None]) & (
            key_pos[None, :] <= query_pos[:, None]
        )
        scores = (
            jnp.einsum(
                "phe,te->hpt", queries, kv_block[:, :HEAD], preferred_element_type=jnp.float32
            )
            * scaling
        )
        return (scores, allowed)

    def tile_stats(kv_block, key_first):
        scores, allowed = tile_scores(kv_block, key_first)
        row_max = jnp.max(jnp.where(allowed[None], scores, -jnp.inf), axis=2)
        row_total = jnp.sum(
            jnp.where(allowed[None], jnp.exp(scores - row_max[:, :, None]), 0.0), axis=2
        )
        return (row_max, row_total)

    empty_max = jnp.full((HEADS, rows_here), -jnp.inf, jnp.float32)
    empty_total = jnp.zeros((HEADS, rows_here), jnp.float32)

    def skip_stats(kv_block):
        return (empty_max, empty_total)

    row_max, row_total = tile_stats(received[0], key_firsts[0])
    for offset in range(1, SPAN):
        other_max, other_total = lax.cond(
            active_list[offset],
            partial(tile_stats, key_first=key_firsts[offset]),
            skip_stats,
            received[offset],
        )
        joined = jnp.maximum(row_max, other_max)
        row_total = row_total * jnp.exp(row_max - joined) + other_total * jnp.exp(
            other_max - joined
        )
        row_max = joined
    log_total = row_max + jnp.log(row_total)

    def tile_probs(kv_block, key_first):
        scores, allowed = tile_scores(kv_block, key_first)
        return jnp.where(allowed[None], jnp.exp(scores - log_total[:, :, None]), 0.0)

    def tile_mix(kv_block, key_first):
        weights = tile_probs(kv_block, key_first).astype(jnp.bfloat16)
        return jnp.einsum(
            "hpt,te->phe", weights, kv_block[:, HEAD:], preferred_element_type=jnp.float32
        )

    zero_mix = jnp.zeros((rows_here, HEADS, HEAD), jnp.float32)

    def skip_mix(kv_block):
        return zero_mix

    mixture = tile_mix(received[0], key_firsts[0])
    for offset in range(1, SPAN):
        mixture = mixture + lax.cond(
            active_list[offset],
            partial(tile_mix, key_first=key_firsts[offset]),
            skip_mix,
            received[offset],
        )
    attended = mixture.astype(jnp.bfloat16)
    row_delta = jnp.einsum(
        "phe,phe->hp", attended_grad, attended, preferred_element_type=jnp.float32
    )

    def tile_backward(kv_block, key_first):
        weights = tile_probs(kv_block, key_first)
        rounded = weights.astype(jnp.bfloat16)
        prob_grad = jnp.einsum(
            "phe,te->hpt", attended_grad, kv_block[:, HEAD:], preferred_element_type=jnp.float32
        )
        score_grad = (weights * (prob_grad - row_delta[:, :, None])).astype(jnp.bfloat16)
        query_grad = (
            jnp.einsum(
                "hpt,te->phe", score_grad, kv_block[:, :HEAD], preferred_element_type=jnp.float32
            )
            * scaling
        )
        key_grad = (
            jnp.einsum("hpt,phe->te", score_grad, queries, preferred_element_type=jnp.float32)
            * scaling
        )
        value_grad = jnp.einsum(
            "hpt,phe->te", rounded, attended_grad, preferred_element_type=jnp.float32
        )
        return (query_grad, jnp.concatenate([key_grad, value_grad], axis=1))

    zero_kv = jnp.zeros((rows_here, 2 * HEAD), jnp.float32)

    def skip_backward(kv_block):
        return (zero_mix, zero_kv)

    query_grad, local_kv = tile_backward(received[0], key_firsts[0])
    kv_terms = [local_kv]
    for offset in range(1, SPAN):
        query_add, kv_add = lax.cond(
            active_list[offset],
            partial(tile_backward, key_first=key_firsts[offset]),
            skip_backward,
            received[offset],
        )
        query_grad = query_grad + query_add
        kv_terms.append(kv_add)
    kv_total = kv_terms[SPAN - 1]
    for offset in range(SPAN - 2, -1, -1):
        kv_total = (
            from_behind(kv_total.astype(jnp.bfloat16), "seq", -1).astype(kv_total.dtype)
            + kv_terms[offset]
        )
    query_pre = rotate_back(query_grad, cosine_table[:, None, :], sine_table[:, None, :]).reshape(
        rows_here, query_width
    )
    key_pre = rotate_back(kv_total[:, :HEAD], cosine_table, sine_table)
    merged_grad = jnp.concatenate([query_pre, key_pre, kv_total[:, HEAD:]], axis=1).astype(
        jnp.bfloat16
    )
    input_grad = lax.dot_general(
        merged_grad, w_qkv, (((1,), (1,)), ((), ())), preferred_element_type=jnp.float32
    ).astype(jnp.bfloat16)[None]
    flat_attended = attended.reshape(rows_here, query_width)
    out_term = lax.dot_general(
        upstream, flat_attended, (((0,), (0,)), ((), ())), preferred_element_type=jnp.float32
    ).astype(jnp.bfloat16)
    qkv_term = lax.dot_general(
        tokens, merged_grad, (((0,), (0,)), ((), ())), preferred_element_type=jnp.float32
    ).astype(jnp.bfloat16)
    qkv_grad, out_rows = reduce_terms(qkv_term, out_term)
    out_grad = out_rows.T
    return (input_grad, qkv_grad, out_grad)


def solution(mesh):
    return jax.shard_map(
        per_device,
        mesh=mesh,
        in_specs=(P("dp", "seq", None), P("dp", "seq", None), P(), P(), P("dp", "seq")),
        out_specs=(P("dp", "seq", None), P(("seq", "dp"), None), P(None, ("seq", "dp"))),
        check_vma=False,
    )
```

```python
import jax
import jax.numpy as jnp
from jax import lax
from jax.experimental import pallas as pl
from jax.experimental.pallas import tpu as pltpu
from jax.sharding import PartitionSpec as P

HEAD = 128
HEADS = 4
SPAN = 4


rope_theta = 500000.0


def from_behind(block, axis, distance):
    devices = range(lax.axis_size(axis))
    route = [(i - distance, i) for i in devices if i - distance in devices]
    return lax.ppermute(block, axis, route)


def rope_tables(offsets):
    half_width = HEAD // 2
    frequency = rope_theta ** (-2.0 * jnp.arange(half_width, dtype=jnp.float32) / HEAD)
    angles = offsets.astype(jnp.float32)[:, None] * frequency[None, :]
    angles = jnp.concatenate([angles, angles], axis=1)
    return (jnp.cos(angles), jnp.sin(angles))


def rotate(vector, cosine_table, sine_table):
    half_width = vector.shape[-1] // 2
    rotated = jnp.concatenate([-vector[..., half_width:], vector[..., :half_width]], axis=-1)
    return vector * cosine_table + rotated * sine_table


def rotate_back(gradient, cosine_table, sine_table):
    half_width = gradient.shape[-1] // 2
    weighted = gradient * sine_table
    return gradient * cosine_table + jnp.concatenate(
        [weighted[..., half_width:], -weighted[..., :half_width]], axis=-1
    )


AXES = 4
ROWS = 32
LANES = 128
STREAMS = 10
BF16 = jnp.bfloat16
F32 = jnp.float32
MESH_ID = pl.DeviceIdType.MESH


def even_pair(i):
    return i + 1 - 2 * (i % 2)


def odd_pair(i):
    return (i + 3 - 2 * (i % 2)) % AXES


def stream_plan(g):
    order = ((0, 1, 2), (1, 2, 0), (2, 0, 1))[g % 3]
    first, second = (even_pair, odd_pair) if (g // 3) % 2 == 0 else (odd_pair, even_pair)
    return order, first, second


def device_of(x, y, z, core):
    return ((((y // 2) * AXES + z) * AXES + x) * 2 + core, y % 2)


def reduce_kernel(q_ref, o_ref, q_out, o_out, q_in, o_in, held, r1a, r1b, r2a, r2b, r3a, r3b, sib_sem, send_sem, recv_sem):
    seq = lax.axis_index("seq")
    dp = lax.axis_index("dp")
    core = seq % 2
    here = ((seq // 2) % AXES, (seq // 32) * 2 + dp, (seq // 8) % AXES)
    sibling = device_of(here[0], here[1], here[2], 1 - core)

    def moved(axis, value):
        spot = list(here)
        spot[axis] = value
        return device_of(*spot, core)

    barrier = pltpu.get_barrier_semaphore()
    pl.semaphore_signal(barrier, inc=1, device_id=sibling, device_id_type=MESH_ID)
    for axis in range(3):
        for pair in (even_pair, odd_pair):
            pl.semaphore_signal(barrier, inc=1, device_id=moved(axis, pair(here[axis])), device_id_type=MESH_ID)
    pl.semaphore_wait(barrier, 7)

    swaps = []
    for n, (src, dst) in enumerate(((q_ref, q_in), (o_ref, o_in))):
        swap = pltpu.make_async_remote_copy(
            src_ref=src.at[:, 1 - core],
            dst_ref=dst,
            send_sem=sib_sem.at[0, n],
            recv_sem=sib_sem.at[1, n],
            device_id=sibling,
            device_id_type=MESH_ID,
        )
        swap.start()
        swaps.append(swap)
    for swap in swaps:
        swap.wait_recv()

    def combine(block, _):
        y_hi = block // 16
        z = (block // 4) % 4
        x = block % 4
        for y_lo in range(2):
            spot = (x, y_hi * 2 + y_lo, z)
            rows = slice(y_lo * ROWS, (y_lo + 1) * ROWS)
            for g in range(STREAMS):
                order, _, _ = stream_plan(g)
                place = (spot[order[0]] * AXES + spot[order[1]]) * AXES + spot[order[2]]
                src, got, col = (q_ref, q_in, g) if g < 6 else (o_ref, o_in, g - 6)
                cols = slice(col * LANES, (col + 1) * LANES)
                total = src[block, core, rows, cols].astype(F32) + got[block, rows, cols].astype(F32)
                held[g, place] = total.astype(BF16)
        return 0

    lax.fori_loop(0, 32, combine, 0)

    def copy(src, dst, g, n, target):
        return pltpu.make_async_remote_copy(
            src_ref=src,
            dst_ref=dst,
            send_sem=send_sem.at[g, n],
            recv_sem=recv_sem.at[g, n],
            device_id=target,
            device_id_type=MESH_ID,
        )

    def add_into(dst, dst_at, src, src_at, count):
        def step(k, _):
            dst[dst_at + (k,)] = (dst[dst_at + (k,)].astype(F32) + src[src_at(k)].astype(F32)).astype(BF16)
            return 0

        if count == 1:
            step(0, 0)
        else:
            lax.fori_loop(0, count, step, 0)

    bufs = ((r1a, r1b), (r2a, r2b), (r3a, r3b))
    sizes = (16, 4, 1)
    sends = {}

    def source(g, stage):
        if stage == 0:
            return held, g
        return bufs[stage - 1][1], g

    def start_first(g, stage):
        order, first, second = stream_plan(g)
        i = here[order[stage]]
        size = sizes[stage]
        f = first(i)
        src, _ = source(g, stage)
        for slot, index in ((1, second(f)), (0, f)):
            sends[g, stage, slot] = copy(
                src.at[g, pl.ds(index * size, size)],
                bufs[stage][0].at[g, slot],
                g,
                stage * 3 + slot,
                moved(order[stage], f),
            )
            sends[g, stage, slot].start()

    for g in range(STREAMS):
        start_first(g, 0)
    for stage in range(3):
        size = sizes[stage]
        for g in range(STREAMS):
            order, first, second = stream_plan(g)
            i = here[order[stage]]
            s = second(i)
            src, _ = source(g, stage)
            sends[g, stage, 1].wait_recv()
            add_into(bufs[stage][0], (g, 1), src, lambda k, s=s, g=g: (g, s * size + k), size)
            sends[g, stage, 2] = copy(bufs[stage][0].at[g, 1], bufs[stage][1].at[g], g, stage * 3 + 2, moved(order[stage], s))
            sends[g, stage, 2].start()
            sends[g, stage, 0].wait_recv()
            add_into(bufs[stage][0], (g, 0), src, lambda k, i=i, g=g: (g, i * size + k), size)
        for g in range(STREAMS):
            sends[g, stage, 2].wait_recv()
            if stage < 2:
                add_into(bufs[stage][1], (g,), bufs[stage][0], lambda k, g=g: (g, 0, k), size)
                start_first(g, stage + 1)
            else:
                total = r3b[g, 0].astype(F32) + r3a[g, 0, 0].astype(F32)
                if g < 6:
                    q_out[:, g * LANES : (g + 1) * LANES] = total
                else:
                    o_out[:, (g - 6) * LANES : (g - 5) * LANES] = total
    for swap in swaps:
        swap.wait_send()
    for send in sends.values():
        send.wait_send()


def reduce_terms(q_term, o_term):
    vmem = pl.BlockSpec(memory_space=pltpu.VMEM)
    tile = (ROWS, LANES)
    return pl.pallas_call(
        reduce_kernel,
        out_shape=(
            jax.ShapeDtypeStruct((ROWS, 768), F32),
            jax.ShapeDtypeStruct((ROWS, 512), F32),
        ),
        in_specs=[vmem, vmem],
        out_specs=(vmem, vmem),
        scratch_shapes=[
            pltpu.VMEM((32, 2 * ROWS, 768), BF16),
            pltpu.VMEM((32, 2 * ROWS, 512), BF16),
            pltpu.VMEM((STREAMS, 64) + tile, BF16),
            pltpu.VMEM((STREAMS, 2, 16) + tile, BF16),
            pltpu.VMEM((STREAMS, 16) + tile, BF16),
            pltpu.VMEM((STREAMS, 2, 4) + tile, BF16),
            pltpu.VMEM((STREAMS, 4) + tile, BF16),
            pltpu.VMEM((STREAMS, 2, 1) + tile, BF16),
            pltpu.VMEM((STREAMS, 1) + tile, BF16),
            pltpu.SemaphoreType.DMA((2, 2)),
            pltpu.SemaphoreType.DMA((STREAMS, 9)),
            pltpu.SemaphoreType.DMA((STREAMS, 9)),
        ],
        compiler_params=pltpu.CompilerParams(
            collective_id=0, has_side_effects=True, vmem_limit_bytes=60 * 1024 * 1024
        ),
    )(q_term.reshape(32, 2, 2 * ROWS, 768), o_term.reshape(32, 2, 2 * ROWS, 512))


NT = (((1,), (1,)), ((), ()))
NN = (((1,), (0,)), ((), ()))
TN = (((0,), (0,)), ((), ()))
LOG2E = 1.4426950408889634
TOK = 512
QROWS = 256
FAR = -1e30


def mm(a, b, dims):
    return lax.dot_general(a, b, dims, preferred_element_type=F32)


def attention_kernel(first_ref, q_ref, g_ref, kv_ref, start_ref, att_ref, dq_ref, dkv_ref):
    scale = HEAD**-0.5
    c = scale * LOG2E
    dkv_ref[...] = jnp.zeros_like(dkv_ref)
    first = first_ref[0]

    def head(h, _):
        cols = pl.ds(pl.multiple_of(h * HEAD, HEAD), HEAD)
        for block in range(TOK // QROWS):
            rows = slice(block * QROWS, (block + 1) * QROWS)
            q = q_ref[rows, cols]
            g = g_ref[rows, cols]
            start = start_ref[rows, :]
            widths = [(block + 1) * QROWS] + [TOK] * (SPAN - 1)
            scores, bias = [], []
            top = None
            for d in range(SPAN):
                s = mm(q, kv_ref[d, : widths[d], :HEAD], NT)
                if d == 0:
                    col = lax.broadcasted_iota(jnp.int32, s.shape, 1)
                    row = lax.broadcasted_iota(jnp.int32, s.shape, 0) + block * QROWS
                    s = jnp.where((col <= row) & (col >= start - first), s, FAR)
                    b = 0.0
                    top = jnp.max(s, axis=1, keepdims=True)
                else:
                    b = jnp.where(start <= first - d * TOK, 0.0, FAR)
                    top = jnp.maximum(top, jnp.max(s, axis=1, keepdims=True) + b)
                scores.append(s)
                bias.append(b)
            top = top * c
            exps = [jnp.exp2(scores[d] * c + (bias[d] - top)) for d in range(SPAN)]
            inverse = 1.0 / sum(jnp.sum(e, axis=1, keepdims=True) for e in exps)
            probs = [e * inverse for e in exps]
            rounded = [p.astype(BF16) for p in probs]
            att = sum(mm(rounded[d], kv_ref[d, : widths[d], HEAD:], NN) for d in range(SPAN)).astype(BF16)
            att_ref[rows, cols] = att
            delta = jnp.sum(g.astype(F32) * att.astype(F32), axis=1, keepdims=True)
            dq = 0.0
            for d in range(SPAN):
                w = widths[d]
                dp = mm(g, kv_ref[d, :w, HEAD:], NT)
                ds = (probs[d] * (dp - delta)).astype(BF16)
                dq = dq + mm(ds, kv_ref[d, :w, :HEAD], NN)
                dkv_ref[d, :w, :HEAD] += mm(ds, q, TN)
                dkv_ref[d, :w, HEAD:] += mm(rounded[d], g, TN)
            dq_ref[rows, cols] = dq * scale
        return 0

    lax.fori_loop(0, HEADS, head, 0)
    for d in range(SPAN):
        dkv_ref[d, :, :HEAD] = dkv_ref[d, :, :HEAD] * scale


def attention(first, q, g, kv, start):
    vmem = pl.BlockSpec(memory_space=pltpu.VMEM)
    return pl.pallas_call(
        attention_kernel,
        out_shape=(
            jax.ShapeDtypeStruct((TOK, HEADS * HEAD), BF16),
            jax.ShapeDtypeStruct((TOK, HEADS * HEAD), F32),
            jax.ShapeDtypeStruct((SPAN, TOK, 2 * HEAD), F32),
        ),
        in_specs=[pl.BlockSpec(memory_space=pltpu.SMEM)] + [vmem] * 4,
        out_specs=(vmem, vmem, vmem),
        compiler_params=pltpu.CompilerParams(vmem_limit_bytes=48 * 1024 * 1024),
    )(first, q, g, kv, start)


def per_device(inputs, cotangent, w_qkv, w_out, doc_start):
    tokens = inputs[0]
    upstream = cotangent[0]
    query_start = doc_start[0]
    rows_here = tokens.shape[0]
    scaling = HEAD ** (-0.5)
    query_width = HEADS * HEAD
    device_index = lax.axis_index("seq")
    query_pos = device_index * rows_here + jnp.arange(rows_here, dtype=jnp.int32)
    cosine_table, sine_table = rope_tables(query_pos - query_start)
    projected = jnp.dot(tokens, w_qkv, preferred_element_type=jnp.float32)
    queries = rotate(
        projected[:, :query_width].reshape(rows_here, HEADS, HEAD),
        cosine_table[:, None, :],
        sine_table[:, None, :],
    ).astype(jnp.bfloat16)
    rotated_keys = rotate(projected[:, query_width : query_width + HEAD], cosine_table, sine_table)
    key_value = jnp.concatenate([rotated_keys, projected[:, query_width + HEAD :]], axis=1).astype(
        jnp.bfloat16
    )
    attended_grad = (
        lax.dot_general(
            upstream, w_out, (((1,), (1,)), ((), ())), preferred_element_type=jnp.float32
        )
        .astype(jnp.bfloat16)
        .reshape(rows_here, HEADS, HEAD)
    )
    received = [key_value]
    travelling = key_value
    for offset in range(1, SPAN):
        travelling = from_behind(travelling, "seq", 1)
        received.append(travelling)
    attended, query_grad, kv_terms = attention(
        (device_index * rows_here).reshape(1),
        queries.reshape(rows_here, query_width),
        attended_grad.reshape(rows_here, query_width),
        jnp.stack(received),
        query_start.reshape(rows_here, 1),
    )
    query_grad = query_grad.reshape(rows_here, HEADS, HEAD)
    kv_total = kv_terms[SPAN - 1]
    for offset in range(SPAN - 2, -1, -1):
        kv_total = (
            from_behind(kv_total.astype(jnp.bfloat16), "seq", -1).astype(kv_total.dtype)
            + kv_terms[offset]
        )
    query_pre = rotate_back(query_grad, cosine_table[:, None, :], sine_table[:, None, :]).reshape(
        rows_here, query_width
    )
    key_pre = rotate_back(kv_total[:, :HEAD], cosine_table, sine_table)
    merged_grad = jnp.concatenate([query_pre, key_pre, kv_total[:, HEAD:]], axis=1).astype(
        jnp.bfloat16
    )
    input_grad = lax.dot_general(
        merged_grad, w_qkv, (((1,), (1,)), ((), ())), preferred_element_type=jnp.float32
    ).astype(jnp.bfloat16)[None]
    flat_attended = attended.reshape(rows_here, query_width)
    out_term = lax.dot_general(
        upstream, flat_attended, (((0,), (0,)), ((), ())), preferred_element_type=jnp.float32
    ).astype(jnp.bfloat16)
    qkv_term = lax.dot_general(
        tokens, merged_grad, (((0,), (0,)), ((), ())), preferred_element_type=jnp.float32
    ).astype(jnp.bfloat16)
    qkv_grad, out_rows = reduce_terms(qkv_term, out_term)
    out_grad = out_rows.T
    return (input_grad, qkv_grad, out_grad)


def solution(mesh):
    return jax.shard_map(
        per_device,
        mesh=mesh,
        in_specs=(P("dp", "seq", None), P("dp", "seq", None), P(), P(), P("dp", "seq")),
        out_specs=(P("dp", "seq", None), P(("seq", "dp"), None), P(None, ("seq", "dp"))),
        check_vma=False,
    )
```

```python
import jax
import jax.numpy as jnp
from jax import lax
from jax.experimental import pallas as pl
from jax.experimental.pallas import tpu as pltpu
from jax.sharding import PartitionSpec as P

HEAD = 128
HEADS = 4
SPAN = 4


rope_theta = 500000.0


def from_behind(block, axis, distance):
    devices = range(lax.axis_size(axis))
    route = [(i - distance, i) for i in devices if i - distance in devices]
    return lax.ppermute(block, axis, route)


def rope_tables(offsets):
    half_width = HEAD // 2
    frequency = rope_theta ** (-2.0 * jnp.arange(half_width, dtype=jnp.float32) / HEAD)
    angles = offsets.astype(jnp.float32)[:, None] * frequency[None, :]
    angles = jnp.concatenate([angles, angles], axis=1)
    return (jnp.cos(angles), jnp.sin(angles))


def rotate(vector, cosine_table, sine_table):
    half_width = vector.shape[-1] // 2
    rotated = jnp.concatenate([-vector[..., half_width:], vector[..., :half_width]], axis=-1)
    return vector * cosine_table + rotated * sine_table


def rotate_back(gradient, cosine_table, sine_table):
    half_width = gradient.shape[-1] // 2
    weighted = gradient * sine_table
    return gradient * cosine_table + jnp.concatenate(
        [weighted[..., half_width:], -weighted[..., :half_width]], axis=-1
    )


AXES = 4
ROWS = 32
LANES = 128
STREAMS = 10
BF16 = jnp.bfloat16
F32 = jnp.float32
MESH_ID = pl.DeviceIdType.MESH


def even_pair(i):
    return i + 1 - 2 * (i % 2)


def odd_pair(i):
    return (i + 3 - 2 * (i % 2)) % AXES


def stream_plan(g):
    order = ((0, 1, 2), (1, 2, 0), (2, 0, 1))[g % 3]
    first, second = (even_pair, odd_pair) if (g // 3) % 2 == 0 else (odd_pair, even_pair)
    return order, first, second


def device_of(x, y, z, core):
    return ((((y // 2) * AXES + z) * AXES + x) * 2 + core, y % 2)


def reduce_kernel(q_ref, o_ref, q_out, o_out, q_in, o_in, held, r1a, r1b, r2a, r2b, r3a, r3b, sib_sem, send_sem, recv_sem):
    seq = lax.axis_index("seq")
    dp = lax.axis_index("dp")
    core = seq % 2
    here = ((seq // 2) % AXES, (seq // 32) * 2 + dp, (seq // 8) % AXES)
    sibling = device_of(here[0], here[1], here[2], 1 - core)

    def moved(axis, value):
        spot = list(here)
        spot[axis] = value
        return device_of(*spot, core)

    barrier = pltpu.get_barrier_semaphore()
    pl.semaphore_signal(barrier, inc=1, device_id=sibling, device_id_type=MESH_ID)
    for axis in range(3):
        for pair in (even_pair, odd_pair):
            pl.semaphore_signal(barrier, inc=1, device_id=moved(axis, pair(here[axis])), device_id_type=MESH_ID)
    pl.semaphore_wait(barrier, 7)

    swaps = []
    for n, (src, dst) in enumerate(((q_ref, q_in), (o_ref, o_in))):
        swap = pltpu.make_async_remote_copy(
            src_ref=src.at[:, 1 - core],
            dst_ref=dst,
            send_sem=sib_sem.at[0, n],
            recv_sem=sib_sem.at[1, n],
            device_id=sibling,
            device_id_type=MESH_ID,
        )
        swap.start()
        swaps.append(swap)
    for swap in swaps:
        swap.wait_recv()

    def combine(block, _):
        y_hi = block // 16
        z = (block // 4) % 4
        x = block % 4
        for y_lo in range(2):
            spot = (x, y_hi * 2 + y_lo, z)
            rows = slice(y_lo * ROWS, (y_lo + 1) * ROWS)
            for g in range(STREAMS):
                order, _, _ = stream_plan(g)
                place = (spot[order[0]] * AXES + spot[order[1]]) * AXES + spot[order[2]]
                src, got, col = (q_ref, q_in, g) if g < 6 else (o_ref, o_in, g - 6)
                cols = slice(col * LANES, (col + 1) * LANES)
                total = src[block, core, rows, cols].astype(F32) + got[block, rows, cols].astype(F32)
                held[g, place] = total.astype(BF16)
        return 0

    lax.fori_loop(0, 32, combine, 0)

    def copy(src, dst, g, n, target):
        return pltpu.make_async_remote_copy(
            src_ref=src,
            dst_ref=dst,
            send_sem=send_sem.at[g, n],
            recv_sem=recv_sem.at[g, n],
            device_id=target,
            device_id_type=MESH_ID,
        )

    def add_into(dst, dst_at, src, src_at):
        total = dst[dst_at].astype(F32) + src[src_at].astype(F32)
        dst[dst_at] = total.astype(BF16)

    bufs = ((r1a, r1b), (r2a, r2b), (r3a, r3b))
    sizes = (16, 4, 1)
    sends = {}

    def source(g, stage):
        if stage == 0:
            return held, g
        return bufs[stage - 1][1], g

    def start_first(g, stage):
        order, first, second = stream_plan(g)
        i = here[order[stage]]
        size = sizes[stage]
        f = first(i)
        src, _ = source(g, stage)
        for slot, index in ((1, second(f)), (0, f)):
            sends[g, stage, slot] = copy(
                src.at[g, pl.ds(index * size, size)],
                bufs[stage][0].at[g, slot],
                g,
                stage * 3 + slot,
                moved(order[stage], f),
            )
            sends[g, stage, slot].start()

    for g in range(STREAMS):
        start_first(g, 0)
    for stage in range(3):
        size = sizes[stage]
        for g in range(STREAMS):
            order, first, second = stream_plan(g)
            i = here[order[stage]]
            s = second(i)
            src, _ = source(g, stage)
            sends[g, stage, 1].wait_recv()
            add_into(bufs[stage][0], (g, 1), src, (g, pl.ds(s * size, size)))
            sends[g, stage, 2] = copy(bufs[stage][0].at[g, 1], bufs[stage][1].at[g], g, stage * 3 + 2, moved(order[stage], s))
            sends[g, stage, 2].start()
            sends[g, stage, 0].wait_recv()
            add_into(bufs[stage][0], (g, 0), src, (g, pl.ds(i * size, size)))
        for g in range(STREAMS):
            sends[g, stage, 2].wait_recv()
            if stage < 2:
                add_into(bufs[stage][1], (g,), bufs[stage][0], (g, 0))
                start_first(g, stage + 1)
            else:
                total = r3b[g, 0].astype(F32) + r3a[g, 0, 0].astype(F32)
                if g < 6:
                    q_out[:, g * LANES : (g + 1) * LANES] = total
                else:
                    o_out[:, (g - 6) * LANES : (g - 5) * LANES] = total
    for swap in swaps:
        swap.wait_send()
    for send in sends.values():
        send.wait_send()


def reduce_terms(q_term, o_term):
    vmem = pl.BlockSpec(memory_space=pltpu.VMEM)
    tile = (ROWS, LANES)
    return pl.pallas_call(
        reduce_kernel,
        out_shape=(
            jax.ShapeDtypeStruct((ROWS, 768), F32),
            jax.ShapeDtypeStruct((ROWS, 512), F32),
        ),
        in_specs=[vmem, vmem],
        out_specs=(vmem, vmem),
        scratch_shapes=[
            pltpu.VMEM((32, 2 * ROWS, 768), BF16),
            pltpu.VMEM((32, 2 * ROWS, 512), BF16),
            pltpu.VMEM((STREAMS, 64) + tile, BF16),
            pltpu.VMEM((STREAMS, 2, 16) + tile, BF16),
            pltpu.VMEM((STREAMS, 16) + tile, BF16),
            pltpu.VMEM((STREAMS, 2, 4) + tile, BF16),
            pltpu.VMEM((STREAMS, 4) + tile, BF16),
            pltpu.VMEM((STREAMS, 2, 1) + tile, BF16),
            pltpu.VMEM((STREAMS, 1) + tile, BF16),
            pltpu.SemaphoreType.DMA((2, 2)),
            pltpu.SemaphoreType.DMA((STREAMS, 9)),
            pltpu.SemaphoreType.DMA((STREAMS, 9)),
        ],
        compiler_params=pltpu.CompilerParams(
            collective_id=0, has_side_effects=True, vmem_limit_bytes=60 * 1024 * 1024
        ),
    )(q_term.reshape(32, 2, 2 * ROWS, 768), o_term.reshape(32, 2, 2 * ROWS, 512))


NT = (((1,), (1,)), ((), ()))
NN = (((1,), (0,)), ((), ()))
TN = (((0,), (0,)), ((), ()))
LOG2E = 1.4426950408889634
TOK = 512
QROWS = 256
FAR = -1e30


def mm(a, b, dims):
    return lax.dot_general(a, b, dims, preferred_element_type=F32)


def attention_kernel(first_ref, q_ref, g_ref, kv_ref, start_ref, att_ref, dq_ref, dkv_ref):
    scale = HEAD**-0.5
    c = scale * LOG2E
    dkv_ref[...] = jnp.zeros_like(dkv_ref)
    first = first_ref[0]

    def head(h, _):
        cols = pl.ds(pl.multiple_of(h * HEAD, HEAD), HEAD)
        for block in range(TOK // QROWS):
            rows = slice(block * QROWS, (block + 1) * QROWS)
            q = q_ref[rows, cols]
            g = g_ref[rows, cols]
            start = start_ref[rows, :]
            widths = [(block + 1) * QROWS] + [TOK] * (SPAN - 1)
            scores, bias = [], []
            top = None
            for d in range(SPAN):
                s = mm(q, kv_ref[d, : widths[d], :HEAD], NT)
                if d == 0:
                    col = lax.broadcasted_iota(jnp.int32, s.shape, 1)
                    row = lax.broadcasted_iota(jnp.int32, s.shape, 0) + block * QROWS
                    s = jnp.where((col <= row) & (col >= start - first), s, FAR)
                    b = 0.0
                    top = jnp.max(s, axis=1, keepdims=True)
                else:
                    b = jnp.where(start <= first - d * TOK, 0.0, FAR)
                    top = jnp.maximum(top, jnp.max(s, axis=1, keepdims=True) + b)
                scores.append(s)
                bias.append(b)
            top = top * c
            exps = [jnp.exp2(scores[d] * c + (bias[d] - top)) for d in range(SPAN)]
            inverse = 1.0 / sum(jnp.sum(e, axis=1, keepdims=True) for e in exps)
            probs = [e * inverse for e in exps]
            rounded = [p.astype(BF16) for p in probs]
            att = sum(mm(rounded[d], kv_ref[d, : widths[d], HEAD:], NN) for d in range(SPAN)).astype(BF16)
            att_ref[rows, cols] = att
            delta = jnp.sum(g.astype(F32) * att.astype(F32), axis=1, keepdims=True)
            dq = 0.0
            for d in range(SPAN):
                w = widths[d]
                dp = mm(g, kv_ref[d, :w, HEAD:], NT)
                ds = (probs[d] * (dp - delta)).astype(BF16)
                dq = dq + mm(ds, kv_ref[d, :w, :HEAD], NN)
                dkv_ref[d, :w, :HEAD] += mm(ds, q, TN)
                dkv_ref[d, :w, HEAD:] += mm(rounded[d], g, TN)
            dq_ref[rows, cols] = dq * scale
        return 0

    lax.fori_loop(0, HEADS, head, 0)
    for d in range(SPAN):
        dkv_ref[d, :, :HEAD] = dkv_ref[d, :, :HEAD] * scale


def attention(first, q, g, kv, start):
    vmem = pl.BlockSpec(memory_space=pltpu.VMEM)
    return pl.pallas_call(
        attention_kernel,
        out_shape=(
            jax.ShapeDtypeStruct((TOK, HEADS * HEAD), BF16),
            jax.ShapeDtypeStruct((TOK, HEADS * HEAD), F32),
            jax.ShapeDtypeStruct((SPAN, TOK, 2 * HEAD), F32),
        ),
        in_specs=[pl.BlockSpec(memory_space=pltpu.SMEM)] + [vmem] * 4,
        out_specs=(vmem, vmem, vmem),
        compiler_params=pltpu.CompilerParams(vmem_limit_bytes=48 * 1024 * 1024),
    )(first, q, g, kv, start)


def per_device(inputs, cotangent, w_qkv, w_out, doc_start):
    tokens = inputs[0]
    upstream = cotangent[0]
    query_start = doc_start[0]
    rows_here = tokens.shape[0]
    scaling = HEAD ** (-0.5)
    query_width = HEADS * HEAD
    device_index = lax.axis_index("seq")
    query_pos = device_index * rows_here + jnp.arange(rows_here, dtype=jnp.int32)
    cosine_table, sine_table = rope_tables(query_pos - query_start)
    projected = jnp.dot(tokens, w_qkv, preferred_element_type=jnp.float32)
    queries = rotate(
        projected[:, :query_width].reshape(rows_here, HEADS, HEAD),
        cosine_table[:, None, :],
        sine_table[:, None, :],
    ).astype(jnp.bfloat16)
    rotated_keys = rotate(projected[:, query_width : query_width + HEAD], cosine_table, sine_table)
    key_value = jnp.concatenate([rotated_keys, projected[:, query_width + HEAD :]], axis=1).astype(
        jnp.bfloat16
    )
    attended_grad = (
        lax.dot_general(
            upstream, w_out, (((1,), (1,)), ((), ())), preferred_element_type=jnp.float32
        )
        .astype(jnp.bfloat16)
        .reshape(rows_here, HEADS, HEAD)
    )
    received = [key_value]
    for offset in range(1, SPAN):
        received.append(from_behind(key_value, "seq", offset))
    attended, query_grad, kv_terms = attention(
        (device_index * rows_here).reshape(1),
        queries.reshape(rows_here, query_width),
        attended_grad.reshape(rows_here, query_width),
        jnp.stack(received),
        query_start.reshape(rows_here, 1),
    )
    query_grad = query_grad.reshape(rows_here, HEADS, HEAD)
    kv_total = kv_terms[0]
    for offset in range(1, SPAN):
        kv_total = kv_total + from_behind(kv_terms[offset].astype(BF16), "seq", -offset).astype(F32)
    query_pre = rotate_back(query_grad, cosine_table[:, None, :], sine_table[:, None, :]).reshape(
        rows_here, query_width
    )
    key_pre = rotate_back(kv_total[:, :HEAD], cosine_table, sine_table)
    merged_grad = jnp.concatenate([query_pre, key_pre, kv_total[:, HEAD:]], axis=1).astype(
        jnp.bfloat16
    )
    input_grad = lax.dot_general(
        merged_grad, w_qkv, (((1,), (1,)), ((), ())), preferred_element_type=jnp.float32
    ).astype(jnp.bfloat16)[None]
    flat_attended = attended.reshape(rows_here, query_width)
    out_term = lax.dot_general(
        upstream, flat_attended, (((0,), (0,)), ((), ())), preferred_element_type=jnp.float32
    ).astype(jnp.bfloat16)
    qkv_term = lax.dot_general(
        tokens, merged_grad, (((0,), (0,)), ((), ())), preferred_element_type=jnp.float32
    ).astype(jnp.bfloat16)
    qkv_grad, out_rows = reduce_terms(qkv_term, out_term)
    out_grad = out_rows.T
    return (input_grad, qkv_grad, out_grad)


def solution(mesh):
    return jax.shard_map(
        per_device,
        mesh=mesh,
        in_specs=(P("dp", "seq", None), P("dp", "seq", None), P(), P(), P("dp", "seq")),
        out_specs=(P("dp", "seq", None), P(("seq", "dp"), None), P(None, ("seq", "dp"))),
        check_vma=False,
    )
```

```python
import jax
import jax.numpy as jnp
from jax import lax
from jax.experimental import pallas as pl
from jax.experimental.pallas import tpu as pltpu
from jax.sharding import PartitionSpec as P

HEAD = 128
HEADS = 4
SPAN = 4


rope_theta = 500000.0


def from_behind(block, axis, distance):
    devices = range(lax.axis_size(axis))
    route = [(i - distance, i) for i in devices if i - distance in devices]
    return lax.ppermute(block, axis, route)


def rope_tables(offsets):
    half_width = HEAD // 2
    frequency = rope_theta ** (-2.0 * jnp.arange(half_width, dtype=jnp.float32) / HEAD)
    angles = offsets.astype(jnp.float32)[:, None] * frequency[None, :]
    angles = jnp.concatenate([angles, angles], axis=1)
    return (jnp.cos(angles), jnp.sin(angles))


def rotate(vector, cosine_table, sine_table):
    half_width = vector.shape[-1] // 2
    rotated = jnp.concatenate([-vector[..., half_width:], vector[..., :half_width]], axis=-1)
    return vector * cosine_table + rotated * sine_table


def rotate_back(gradient, cosine_table, sine_table):
    half_width = gradient.shape[-1] // 2
    weighted = gradient * sine_table
    return gradient * cosine_table + jnp.concatenate(
        [weighted[..., half_width:], -weighted[..., :half_width]], axis=-1
    )


AXES = 4
ROWS = 32
LANES = 128
STREAMS = 10
Q_STREAMS = tuple(range(6))
O_STREAMS = tuple(range(6, 10))
CHUNKS = 4
BF16 = jnp.bfloat16
F32 = jnp.float32
MESH_ID = pl.DeviceIdType.MESH


def even_pair(i):
    return i + 1 - 2 * (i % 2)


def odd_pair(i):
    return (i + 3 - 2 * (i % 2)) % AXES


def stream_plan(g):
    order = ((0, 1, 2), (1, 2, 0), (2, 0, 1))[g % 3]
    first, second = (even_pair, odd_pair) if (g // 3) % 2 == 0 else (odd_pair, even_pair)
    return order, first, second


def device_of(x, y, z, core):
    return ((((y // 2) * AXES + z) * AXES + x) * 2 + core, y % 2)


def reduce_kernel(tok_ref, mg_ref, o_ref, q_out, o_out, q_ref, q_in, o_in, held, r1a, r1b, r2a, r2b, r3a, r3b, sib_sem, send_sem, recv_sem):
    seq = lax.axis_index("seq")
    dp = lax.axis_index("dp")
    core = seq % 2
    here = ((seq // 2) % AXES, (seq // 32) * 2 + dp, (seq // 8) % AXES)
    sibling = device_of(here[0], here[1], here[2], 1 - core)

    def moved(axis, value):
        spot = list(here)
        spot[axis] = value
        return device_of(*spot, core)

    barrier = pltpu.get_barrier_semaphore()
    pl.semaphore_signal(barrier, inc=1, device_id=sibling, device_id_type=MESH_ID)
    for axis in range(3):
        for pair in (even_pair, odd_pair):
            pl.semaphore_signal(barrier, inc=1, device_id=moved(axis, pair(here[axis])), device_id_type=MESH_ID)

    span = 2 * AXES * AXES // CHUNKS

    def multiply(chunk):
        def pair(k, _):
            at = chunk * span + 2 * k
            cols = pl.ds(pl.multiple_of(at * 4 * ROWS, 8 * ROWS), 8 * ROWS)
            term = mm(tok_ref[:, cols], mg_ref[...], TN).astype(BF16)
            q_ref[pl.ds(at, 2)] = term.reshape(2, 2, 2 * ROWS, 768)
            return 0

        lax.fori_loop(0, span // 2, pair, 0)

    def swap(n, src, dst):
        return pltpu.make_async_remote_copy(
            src_ref=src,
            dst_ref=dst,
            send_sem=sib_sem.at[0, n],
            recv_sem=sib_sem.at[1, n],
            device_id=sibling,
            device_id_type=MESH_ID,
        )

    def combine(own, got, streams, start, count):
        def step(k, _):
            block = start + k
            y_hi = block // 16
            z = (block // 4) % 4
            x = block % 4
            for y_lo in range(2):
                spot = (x, y_hi * 2 + y_lo, z)
                rows = slice(y_lo * ROWS, (y_lo + 1) * ROWS)
                for g in streams:
                    order, _, _ = stream_plan(g)
                    place = (spot[order[0]] * AXES + spot[order[1]]) * AXES + spot[order[2]]
                    col = g - streams[0]
                    cols = slice(col * LANES, (col + 1) * LANES)
                    total = own[block, core, rows, cols].astype(F32) + got[block, rows, cols].astype(F32)
                    held[g, place] = total.astype(BF16)
            return 0

        lax.fori_loop(0, count, step, 0)

    def copy(src, dst, g, n, target):
        return pltpu.make_async_remote_copy(
            src_ref=src,
            dst_ref=dst,
            send_sem=send_sem.at[g, n],
            recv_sem=recv_sem.at[g, n],
            device_id=target,
            device_id_type=MESH_ID,
        )

    def add_into(dst, dst_at, src, src_at):
        total = dst[dst_at].astype(F32) + src[src_at].astype(F32)
        dst[dst_at] = total.astype(BF16)

    bufs = ((r1a, r1b), (r2a, r2b), (r3a, r3b))
    sizes = (16, 4, 1)
    sends = {}

    def source(g, stage):
        if stage == 0:
            return held, g
        return bufs[stage - 1][1], g

    def start_first(g, stage):
        order, first, second = stream_plan(g)
        i = here[order[stage]]
        size = sizes[stage]
        f = first(i)
        src, _ = source(g, stage)
        for slot, index in ((1, second(f)), (0, f)):
            sends[g, stage, slot] = copy(
                src.at[g, pl.ds(index * size, size)],
                bufs[stage][0].at[g, slot],
                g,
                stage * 3 + slot,
                moved(order[stage], f),
            )
            sends[g, stage, slot].start()

    swaps = []
    for chunk in range(CHUNKS):
        multiply(chunk)
        if chunk == 0:
            pl.semaphore_wait(barrier, 7)
            swaps.append(swap(CHUNKS, o_ref.at[:, 1 - core], o_in))
            swaps[0].start()
        part = pl.ds(chunk * span, span)
        swaps.append(swap(chunk, q_ref.at[part, 1 - core], q_in.at[part]))
        swaps[-1].start()
        if chunk == 1:
            swaps[0].wait_recv()
            combine(o_ref, o_in, O_STREAMS, 0, 2 * AXES * AXES)
            for g in O_STREAMS:
                start_first(g, 0)
    for chunk in range(CHUNKS):
        swaps[1 + chunk].wait_recv()
        combine(q_ref, q_in, Q_STREAMS, chunk * span, span)
    for g in Q_STREAMS:
        start_first(g, 0)
    for stage in range(3):
        size = sizes[stage]
        for g in O_STREAMS + Q_STREAMS:
            order, first, second = stream_plan(g)
            i = here[order[stage]]
            s = second(i)
            src, _ = source(g, stage)
            sends[g, stage, 1].wait_recv()
            add_into(bufs[stage][0], (g, 1), src, (g, pl.ds(s * size, size)))
            sends[g, stage, 2] = copy(bufs[stage][0].at[g, 1], bufs[stage][1].at[g], g, stage * 3 + 2, moved(order[stage], s))
            sends[g, stage, 2].start()
            sends[g, stage, 0].wait_recv()
            add_into(bufs[stage][0], (g, 0), src, (g, pl.ds(i * size, size)))
        for g in O_STREAMS + Q_STREAMS:
            sends[g, stage, 2].wait_recv()
            if stage < 2:
                add_into(bufs[stage][1], (g,), bufs[stage][0], (g, 0))
                start_first(g, stage + 1)
            else:
                total = r3b[g, 0].astype(F32) + r3a[g, 0, 0].astype(F32)
                if g < 6:
                    q_out[:, g * LANES : (g + 1) * LANES] = total
                else:
                    o_out[:, (g - 6) * LANES : (g - 5) * LANES] = total
    for item in swaps:
        item.wait_send()
    for send in sends.values():
        send.wait_send()


def reduce_terms(tokens, merged_grad, o_term):
    vmem = pl.BlockSpec(memory_space=pltpu.VMEM)
    tile = (ROWS, LANES)
    return pl.pallas_call(
        reduce_kernel,
        out_shape=(
            jax.ShapeDtypeStruct((ROWS, 768), F32),
            jax.ShapeDtypeStruct((ROWS, 512), F32),
        ),
        in_specs=[vmem, vmem, vmem],
        out_specs=(vmem, vmem),
        scratch_shapes=[
            pltpu.VMEM((32, 2, 2 * ROWS, 768), BF16),
            pltpu.VMEM((32, 2 * ROWS, 768), BF16),
            pltpu.VMEM((32, 2 * ROWS, 512), BF16),
            pltpu.VMEM((STREAMS, 64) + tile, BF16),
            pltpu.VMEM((STREAMS, 2, 16) + tile, BF16),
            pltpu.VMEM((STREAMS, 16) + tile, BF16),
            pltpu.VMEM((STREAMS, 2, 4) + tile, BF16),
            pltpu.VMEM((STREAMS, 4) + tile, BF16),
            pltpu.VMEM((STREAMS, 2, 1) + tile, BF16),
            pltpu.VMEM((STREAMS, 1) + tile, BF16),
            pltpu.SemaphoreType.DMA((2, CHUNKS + 1)),
            pltpu.SemaphoreType.DMA((STREAMS, 9)),
            pltpu.SemaphoreType.DMA((STREAMS, 9)),
        ],
        compiler_params=pltpu.CompilerParams(
            collective_id=0, has_side_effects=True, vmem_limit_bytes=60 * 1024 * 1024
        ),
    )(tokens, merged_grad, o_term.reshape(32, 2, 2 * ROWS, 512))


NT = (((1,), (1,)), ((), ()))
NN = (((1,), (0,)), ((), ()))
TN = (((0,), (0,)), ((), ()))
LOG2E = 1.4426950408889634
TOK = 512
QROWS = 256
FAR = -1e30


def mm(a, b, dims):
    return lax.dot_general(a, b, dims, preferred_element_type=F32)


def attention_kernel(first_ref, q_ref, g_ref, kv_ref, start_ref, att_ref, dq_ref, dkv_ref):
    scale = HEAD**-0.5
    c = scale * LOG2E
    dkv_ref[...] = jnp.zeros_like(dkv_ref)
    first = first_ref[0]

    def head(h, _):
        cols = pl.ds(pl.multiple_of(h * HEAD, HEAD), HEAD)
        for block in range(TOK // QROWS):
            rows = slice(block * QROWS, (block + 1) * QROWS)
            q = q_ref[rows, cols]
            g = g_ref[rows, cols]
            start = start_ref[rows, :]
            widths = [(block + 1) * QROWS] + [TOK] * (SPAN - 1)
            scores, bias = [], []
            top = None
            for d in range(SPAN):
                s = mm(q, kv_ref[d, : widths[d], :HEAD], NT)
                if d == 0:
                    col = lax.broadcasted_iota(jnp.int32, s.shape, 1)
                    row = lax.broadcasted_iota(jnp.int32, s.shape, 0) + block * QROWS
                    s = jnp.where((col <= row) & (col >= start - first), s, FAR)
                    b = 0.0
                    top = jnp.max(s, axis=1, keepdims=True)
                else:
                    b = jnp.where(start <= first - d * TOK, 0.0, FAR)
                    top = jnp.maximum(top, jnp.max(s, axis=1, keepdims=True) + b)
                scores.append(s)
                bias.append(b)
            top = top * c
            exps = [jnp.exp2(scores[d] * c + (bias[d] - top)) for d in range(SPAN)]
            inverse = 1.0 / sum(jnp.sum(e, axis=1, keepdims=True) for e in exps)
            probs = [e * inverse for e in exps]
            rounded = [p.astype(BF16) for p in probs]
            att = sum(mm(rounded[d], kv_ref[d, : widths[d], HEAD:], NN) for d in range(SPAN)).astype(BF16)
            att_ref[rows, cols] = att
            delta = jnp.sum(g.astype(F32) * att.astype(F32), axis=1, keepdims=True)
            dq = 0.0
            for d in range(SPAN):
                w = widths[d]
                dp = mm(g, kv_ref[d, :w, HEAD:], NT)
                ds = (probs[d] * (dp - delta)).astype(BF16)
                dq = dq + mm(ds, kv_ref[d, :w, :HEAD], NN)
                dkv_ref[d, :w, :HEAD] += mm(ds, q, TN)
                dkv_ref[d, :w, HEAD:] += mm(rounded[d], g, TN)
            dq_ref[rows, cols] = dq * scale
        return 0

    lax.fori_loop(0, HEADS, head, 0)
    for d in range(SPAN):
        dkv_ref[d, :, :HEAD] = dkv_ref[d, :, :HEAD] * scale


def attention(first, q, g, kv, start):
    vmem = pl.BlockSpec(memory_space=pltpu.VMEM)
    return pl.pallas_call(
        attention_kernel,
        out_shape=(
            jax.ShapeDtypeStruct((TOK, HEADS * HEAD), BF16),
            jax.ShapeDtypeStruct((TOK, HEADS * HEAD), F32),
            jax.ShapeDtypeStruct((SPAN, TOK, 2 * HEAD), F32),
        ),
        in_specs=[pl.BlockSpec(memory_space=pltpu.SMEM)] + [vmem] * 4,
        out_specs=(vmem, vmem, vmem),
        compiler_params=pltpu.CompilerParams(vmem_limit_bytes=48 * 1024 * 1024),
    )(first, q, g, kv, start)


def out_kernel(g_ref, att_ref, term_ref):
    term_ref[...] = mm(g_ref[...], att_ref[...], TN).astype(BF16)


def out_terms(upstream, attended):
    rows, width = upstream.shape
    cols = attended.shape[1]
    step = 512
    return pl.pallas_call(
        out_kernel,
        grid=(width // step,),
        out_shape=jax.ShapeDtypeStruct((width, cols), BF16),
        in_specs=[
            pl.BlockSpec((rows, step), lambda i: (0, i)),
            pl.BlockSpec((rows, cols), lambda i: (0, 0)),
        ],
        out_specs=pl.BlockSpec((step, cols), lambda i: (i, 0)),
        cost_estimate=pl.CostEstimate(
            flops=2 * rows * width * cols,
            bytes_accessed=2 * (rows * width + rows * cols + width * cols),
            transcendentals=0,
        ),
    )(upstream, attended)


def per_device(inputs, cotangent, w_qkv, w_out, doc_start):
    tokens = inputs[0]
    upstream = cotangent[0]
    query_start = doc_start[0]
    rows_here = tokens.shape[0]
    scaling = HEAD ** (-0.5)
    query_width = HEADS * HEAD
    device_index = lax.axis_index("seq")
    query_pos = device_index * rows_here + jnp.arange(rows_here, dtype=jnp.int32)
    cosine_table, sine_table = rope_tables(query_pos - query_start)
    projected = jnp.dot(tokens, w_qkv, preferred_element_type=jnp.float32)
    queries = rotate(
        projected[:, :query_width].reshape(rows_here, HEADS, HEAD),
        cosine_table[:, None, :],
        sine_table[:, None, :],
    ).astype(jnp.bfloat16)
    rotated_keys = rotate(projected[:, query_width : query_width + HEAD], cosine_table, sine_table)
    key_value = jnp.concatenate([rotated_keys, projected[:, query_width + HEAD :]], axis=1).astype(
        jnp.bfloat16
    )
    attended_grad = (
        lax.dot_general(
            upstream, w_out, (((1,), (1,)), ((), ())), preferred_element_type=jnp.float32
        )
        .astype(jnp.bfloat16)
        .reshape(rows_here, HEADS, HEAD)
    )
    received = [key_value]
    for offset in range(1, SPAN):
        received.append(from_behind(key_value, "seq", offset))
    attended, query_grad, kv_terms = attention(
        (device_index * rows_here).reshape(1),
        queries.reshape(rows_here, query_width),
        attended_grad.reshape(rows_here, query_width),
        jnp.stack(received),
        query_start.reshape(rows_here, 1),
    )
    query_grad = query_grad.reshape(rows_here, HEADS, HEAD)
    kv_total = kv_terms[0]
    for offset in range(1, SPAN):
        kv_total = kv_total + from_behind(kv_terms[offset].astype(BF16), "seq", -offset).astype(F32)
    query_pre = rotate_back(query_grad, cosine_table[:, None, :], sine_table[:, None, :]).reshape(
        rows_here, query_width
    )
    key_pre = rotate_back(kv_total[:, :HEAD], cosine_table, sine_table)
    merged_grad = jnp.concatenate([query_pre, key_pre, kv_total[:, HEAD:]], axis=1).astype(
        jnp.bfloat16
    )
    input_grad = lax.dot_general(
        merged_grad, w_qkv, (((1,), (1,)), ((), ())), preferred_element_type=jnp.float32
    ).astype(jnp.bfloat16)[None]
    flat_attended = attended.reshape(rows_here, query_width)
    out_term = out_terms(upstream, flat_attended)
    qkv_grad, out_rows = reduce_terms(tokens, merged_grad, out_term)
    out_grad = out_rows.T
    return (input_grad, qkv_grad, out_grad)


def solution(mesh):
    return jax.shard_map(
        per_device,
        mesh=mesh,
        in_specs=(P("dp", "seq", None), P("dp", "seq", None), P(), P(), P("dp", "seq")),
        out_specs=(P("dp", "seq", None), P(("seq", "dp"), None), P(None, ("seq", "dp"))),
        check_vma=False,
    )
```

```python
import jax
import jax.numpy as jnp
from jax import lax
from jax.experimental import pallas as pl
from jax.experimental.pallas import tpu as pltpu
from jax.sharding import PartitionSpec as P

HEAD = 128
HEADS = 4
SPAN = 4


rope_theta = 500000.0


def rope_tables(offsets):
    half_width = HEAD // 2
    frequency = rope_theta ** (-2.0 * jnp.arange(half_width, dtype=jnp.float32) / HEAD)
    angles = offsets.astype(jnp.float32)[:, None] * frequency[None, :]
    cosine, sine = jnp.cos(angles), jnp.sin(angles)
    return (jnp.concatenate([cosine, cosine], axis=1), jnp.concatenate([-sine, sine], axis=1))


AXES = 4
ROWS = 32
LANES = 128
STREAMS = 10
Q_STREAMS = tuple(range(6))
O_STREAMS = tuple(range(6, 10))
CHUNKS = 4
BF16 = jnp.bfloat16
F32 = jnp.float32
MESH_ID = pl.DeviceIdType.MESH


def even_pair(i):
    return i + 1 - 2 * (i % 2)


def odd_pair(i):
    return (i + 3 - 2 * (i % 2)) % AXES


def stream_plan(g):
    order = ((0, 1, 2), (1, 2, 0), (2, 0, 1))[g % 3]
    first, second = (even_pair, odd_pair) if (g // 3) % 2 == 0 else (odd_pair, even_pair)
    return order, first, second


def device_of(x, y, z, core):
    return ((((y // 2) * AXES + z) * AXES + x) * 2 + core, y % 2)


def reduce_kernel(tok_ref, mg_ref, o_ref, q_out, o_out, q_ref, q_in, o_in, held, r1a, r1b, r2a, r2b, r3a, r3b, sib_sem, send_sem, recv_sem):
    seq = lax.axis_index("seq")
    dp = lax.axis_index("dp")
    core = seq % 2
    here = ((seq // 2) % AXES, (seq // 32) * 2 + dp, (seq // 8) % AXES)
    sibling = device_of(here[0], here[1], here[2], 1 - core)

    def moved(axis, value):
        spot = list(here)
        spot[axis] = value
        return device_of(*spot, core)

    barrier = pltpu.get_barrier_semaphore()
    pl.semaphore_signal(barrier, inc=1, device_id=sibling, device_id_type=MESH_ID)
    for axis in range(3):
        for pair in (even_pair, odd_pair):
            pl.semaphore_signal(barrier, inc=1, device_id=moved(axis, pair(here[axis])), device_id_type=MESH_ID)

    span = 2 * AXES * AXES // CHUNKS

    def multiply(chunk):
        def pair(k, _):
            at = chunk * span + 2 * k
            cols = pl.ds(pl.multiple_of(at * 4 * ROWS, 8 * ROWS), 8 * ROWS)
            term = mm(tok_ref[:, cols], mg_ref[...], TN).astype(BF16)
            q_ref[pl.ds(at, 2)] = term.reshape(2, 2, 2 * ROWS, 768)
            return 0

        lax.fori_loop(0, span // 2, pair, 0)

    def swap(n, src, dst):
        return pltpu.make_async_remote_copy(
            src_ref=src,
            dst_ref=dst,
            send_sem=sib_sem.at[0, n],
            recv_sem=sib_sem.at[1, n],
            device_id=sibling,
            device_id_type=MESH_ID,
        )

    def combine(own, got, streams, start, count):
        def step(k, _):
            block = start + k
            y_hi = block // 16
            z = (block // 4) % 4
            x = block % 4
            for y_lo in range(2):
                spot = (x, y_hi * 2 + y_lo, z)
                rows = slice(y_lo * ROWS, (y_lo + 1) * ROWS)
                for g in streams:
                    order, _, _ = stream_plan(g)
                    place = (spot[order[0]] * AXES + spot[order[1]]) * AXES + spot[order[2]]
                    col = g - streams[0]
                    cols = slice(col * LANES, (col + 1) * LANES)
                    total = own[block, core, rows, cols].astype(F32) + got[block, rows, cols].astype(F32)
                    held[g, place] = total.astype(BF16)
            return 0

        lax.fori_loop(0, count, step, 0)

    def copy(src, dst, g, n, target):
        return pltpu.make_async_remote_copy(
            src_ref=src,
            dst_ref=dst,
            send_sem=send_sem.at[g, n],
            recv_sem=recv_sem.at[g, n],
            device_id=target,
            device_id_type=MESH_ID,
        )

    def add_into(dst, dst_at, src, src_at):
        total = dst[dst_at].astype(F32) + src[src_at].astype(F32)
        dst[dst_at] = total.astype(BF16)

    bufs = ((r1a, r1b), (r2a, r2b), (r3a, r3b))
    sizes = (16, 4, 1)
    sends = {}

    def source(g, stage):
        if stage == 0:
            return held, g
        return bufs[stage - 1][1], g

    def start_first(g, stage):
        order, first, second = stream_plan(g)
        i = here[order[stage]]
        size = sizes[stage]
        f = first(i)
        src, _ = source(g, stage)
        for slot, index in ((1, second(f)), (0, f)):
            sends[g, stage, slot] = copy(
                src.at[g, pl.ds(index * size, size)],
                bufs[stage][0].at[g, slot],
                g,
                stage * 3 + slot,
                moved(order[stage], f),
            )
            sends[g, stage, slot].start()

    swaps = []
    for chunk in range(CHUNKS):
        multiply(chunk)
        if chunk == 0:
            pl.semaphore_wait(barrier, 7)
            swaps.append(swap(CHUNKS, o_ref.at[:, 1 - core], o_in))
            swaps[0].start()
        part = pl.ds(chunk * span, span)
        swaps.append(swap(chunk, q_ref.at[part, 1 - core], q_in.at[part]))
        swaps[-1].start()
        if chunk == 1:
            swaps[0].wait_recv()
            combine(o_ref, o_in, O_STREAMS, 0, 2 * AXES * AXES)
            for g in O_STREAMS:
                start_first(g, 0)
    for chunk in range(CHUNKS):
        swaps[1 + chunk].wait_recv()
        combine(q_ref, q_in, Q_STREAMS, chunk * span, span)
    for g in Q_STREAMS:
        start_first(g, 0)
    for stage in range(3):
        size = sizes[stage]
        for g in O_STREAMS + Q_STREAMS:
            order, first, second = stream_plan(g)
            i = here[order[stage]]
            s = second(i)
            src, _ = source(g, stage)
            sends[g, stage, 1].wait_recv()
            add_into(bufs[stage][0], (g, 1), src, (g, pl.ds(s * size, size)))
            sends[g, stage, 2] = copy(bufs[stage][0].at[g, 1], bufs[stage][1].at[g], g, stage * 3 + 2, moved(order[stage], s))
            sends[g, stage, 2].start()
            sends[g, stage, 0].wait_recv()
            add_into(bufs[stage][0], (g, 0), src, (g, pl.ds(i * size, size)))
        for g in O_STREAMS + Q_STREAMS:
            sends[g, stage, 2].wait_recv()
            if stage < 2:
                add_into(bufs[stage][1], (g,), bufs[stage][0], (g, 0))
                start_first(g, stage + 1)
            else:
                total = r3b[g, 0].astype(F32) + r3a[g, 0, 0].astype(F32)
                if g < 6:
                    q_out[:, g * LANES : (g + 1) * LANES] = total
                else:
                    o_out[:, (g - 6) * LANES : (g - 5) * LANES] = total
    for item in swaps:
        item.wait_send()
    for send in sends.values():
        send.wait_send()


def reduce_terms(tokens, merged_grad, o_term):
    vmem = pl.BlockSpec(memory_space=pltpu.VMEM)
    tile = (ROWS, LANES)
    return pl.pallas_call(
        reduce_kernel,
        out_shape=(
            jax.ShapeDtypeStruct((ROWS, 768), F32),
            jax.ShapeDtypeStruct((ROWS, 512), F32),
        ),
        in_specs=[vmem, vmem, vmem],
        out_specs=(vmem, vmem),
        scratch_shapes=[
            pltpu.VMEM((32, 2, 2 * ROWS, 768), BF16),
            pltpu.VMEM((32, 2 * ROWS, 768), BF16),
            pltpu.VMEM((32, 2 * ROWS, 512), BF16),
            pltpu.VMEM((STREAMS, 64) + tile, BF16),
            pltpu.VMEM((STREAMS, 2, 16) + tile, BF16),
            pltpu.VMEM((STREAMS, 16) + tile, BF16),
            pltpu.VMEM((STREAMS, 2, 4) + tile, BF16),
            pltpu.VMEM((STREAMS, 4) + tile, BF16),
            pltpu.VMEM((STREAMS, 2, 1) + tile, BF16),
            pltpu.VMEM((STREAMS, 1) + tile, BF16),
            pltpu.SemaphoreType.DMA((2, CHUNKS + 1)),
            pltpu.SemaphoreType.DMA((STREAMS, 9)),
            pltpu.SemaphoreType.DMA((STREAMS, 9)),
        ],
        compiler_params=pltpu.CompilerParams(
            collective_id=0, has_side_effects=True, vmem_limit_bytes=60 * 1024 * 1024
        ),
    )(tokens, merged_grad, o_term.reshape(32, 2, 2 * ROWS, 512))


NT = (((1,), (1,)), ((), ()))
NN = (((1,), (0,)), ((), ()))
TN = (((0,), (0,)), ((), ()))
LOG2E = 1.4426950408889634
TOK = 512
QROWS = 256
FAR = -1e30


def mm(a, b, dims):
    return lax.dot_general(a, b, dims, preferred_element_type=F32)


def middle_kernel(
    proj_ref, up_ref, w_ref, start_ref, cos_ref, sin_ref, merged_ref, term_ref,
    kv_ref, g_ref, att_ref, dkv_ref, far_ref, back_ref, send_sem, recv_sem,
):
    scale = HEAD**-0.5
    c = scale * LOG2E
    width = HEADS * HEAD
    seq = lax.axis_index("seq")
    dp_index = lax.axis_index("dp")
    count = lax.axis_size("seq")
    first = seq * TOK

    def peer(distance):
        return (lax.rem(seq + distance + count, count), dp_index)

    barrier = pltpu.get_barrier_semaphore()
    for d in range(1, SPAN):
        for distance in (d, -d):
            pl.semaphore_signal(barrier, inc=1, device_id=peer(distance), device_id_type=MESH_ID)

    def turn(v, rows):
        return v * cos_ref[rows, :] + pltpu.roll(v, HEAD // 2, 1) * sin_ref[rows, :]

    def turn_back(v, rows):
        return v * cos_ref[rows, :] + pltpu.roll(v * sin_ref[rows, :], HEAD // 2, 1)

    everything = slice(0, TOK)
    kv_ref[0, :, :HEAD] = turn(proj_ref[:, width : width + HEAD], everything).astype(BF16)
    kv_ref[0, :, HEAD:] = proj_ref[:, width + HEAD :].astype(BF16)
    dkv_ref[...] = jnp.zeros_like(dkv_ref)
    pl.semaphore_wait(barrier, 2 * (SPAN - 1))

    def copy(n, src, dst, distance):
        return pltpu.make_async_remote_copy(
            src_ref=src,
            dst_ref=dst,
            send_sem=send_sem.at[n],
            recv_sem=recv_sem.at[n],
            device_id=peer(distance),
            device_id_type=MESH_ID,
        )

    ahead = [copy(d - 1, kv_ref.at[0], kv_ref.at[d], d) for d in range(1, SPAN)]
    for item in ahead:
        item.start()
    for block in range(TOK // QROWS):
        rows = slice(block * QROWS, (block + 1) * QROWS)
        g_ref[rows, :] = mm(up_ref[rows, :], w_ref[...], NT).astype(BF16)
    for item in ahead:
        item.wait_recv()

    def head(h, _):
        cols = pl.ds(pl.multiple_of(h * HEAD, HEAD), HEAD)
        for block in range(TOK // QROWS):
            rows = slice(block * QROWS, (block + 1) * QROWS)
            q = turn(proj_ref[rows, cols], rows).astype(BF16)
            g = g_ref[rows, cols]
            start = start_ref[rows, :]
            widths = [(block + 1) * QROWS] + [TOK] * (SPAN - 1)
            scores, bias = [], []
            top = None
            for d in range(SPAN):
                s = mm(q, kv_ref[d, : widths[d], :HEAD], NT)
                if d == 0:
                    col = lax.broadcasted_iota(jnp.int32, s.shape, 1)
                    row = lax.broadcasted_iota(jnp.int32, s.shape, 0) + block * QROWS
                    s = jnp.where((col <= row) & (col >= start - first), s, FAR)
                    b = 0.0
                    top = jnp.max(s, axis=1, keepdims=True)
                else:
                    b = jnp.where(start <= first - d * TOK, 0.0, FAR)
                    top = jnp.maximum(top, jnp.max(s, axis=1, keepdims=True) + b)
                scores.append(s)
                bias.append(b)
            top = top * c
            exps = [jnp.exp2(scores[d] * c + (bias[d] - top)) for d in range(SPAN)]
            inverse = 1.0 / sum(jnp.sum(e, axis=1, keepdims=True) for e in exps)
            probs = [e * inverse for e in exps]
            rounded = [p.astype(BF16) for p in probs]
            att = sum(mm(rounded[d], kv_ref[d, : widths[d], HEAD:], NN) for d in range(SPAN)).astype(BF16)
            att_ref[rows, cols] = att
            delta = jnp.sum(g.astype(F32) * att.astype(F32), axis=1, keepdims=True)
            dq = 0.0
            for d in range(SPAN):
                w = widths[d]
                dp = mm(g, kv_ref[d, :w, HEAD:], NT)
                ds = (probs[d] * (dp - delta)).astype(BF16)
                dq = dq + mm(ds, kv_ref[d, :w, :HEAD], NN)
                dkv_ref[d, :w, :HEAD] += mm(ds, q, TN)
                dkv_ref[d, :w, HEAD:] += mm(rounded[d], g, TN)
            merged_ref[rows, cols] = turn_back(dq * scale, rows).astype(BF16)
        return 0

    lax.fori_loop(0, HEADS, head, 0)
    for d in range(1, SPAN):
        far_ref[d - 1, :, :HEAD] = (dkv_ref[d, :, :HEAD] * scale).astype(BF16)
        far_ref[d - 1, :, HEAD:] = dkv_ref[d, :, HEAD:].astype(BF16)
    behind = [copy(SPAN - 2 + d, far_ref.at[d - 1], back_ref.at[d - 1], -d) for d in range(1, SPAN)]
    for item in behind:
        item.start()

    def term(i, _):
        cols = pl.ds(pl.multiple_of(i * TOK, TOK), TOK)
        term_ref[cols, :] = mm(up_ref[:, cols], att_ref[...], TN).astype(BF16)
        return 0

    lax.fori_loop(0, up_ref.shape[1] // TOK, term, 0)
    for item in behind:
        item.wait_recv()
    key = dkv_ref[0, :, :HEAD] * scale
    value = dkv_ref[0, :, HEAD:]
    for d in range(SPAN - 1):
        key = key + back_ref[d, :, :HEAD].astype(F32)
        value = value + back_ref[d, :, HEAD:].astype(F32)
    merged_ref[:, width : width + HEAD] = turn_back(key, everything).astype(BF16)
    merged_ref[:, width + HEAD :] = value.astype(BF16)
    for item in ahead + behind:
        item.wait_send()


def middle(projected, upstream, w_out, start, cosine, sine):
    vmem = pl.BlockSpec(memory_space=pltpu.VMEM)
    width = HEADS * HEAD
    return pl.pallas_call(
        middle_kernel,
        out_shape=(
            jax.ShapeDtypeStruct((TOK, width + 2 * HEAD), BF16),
            jax.ShapeDtypeStruct((upstream.shape[1], width), BF16),
        ),
        in_specs=[vmem] * 6,
        out_specs=(vmem, vmem),
        scratch_shapes=[
            pltpu.VMEM((SPAN, TOK, 2 * HEAD), BF16),
            pltpu.VMEM((TOK, width), BF16),
            pltpu.VMEM((TOK, width), BF16),
            pltpu.VMEM((SPAN, TOK, 2 * HEAD), F32),
            pltpu.VMEM((SPAN - 1, TOK, 2 * HEAD), BF16),
            pltpu.VMEM((SPAN - 1, TOK, 2 * HEAD), BF16),
            pltpu.SemaphoreType.DMA((2 * (SPAN - 1),)),
            pltpu.SemaphoreType.DMA((2 * (SPAN - 1),)),
        ],
        compiler_params=pltpu.CompilerParams(
            collective_id=1, has_side_effects=True, vmem_limit_bytes=60 * 1024 * 1024
        ),
    )(projected, upstream, w_out, start, cosine, sine)


def per_device(inputs, cotangent, w_qkv, w_out, doc_start):
    tokens = inputs[0]
    query_start = doc_start[0]
    rows_here = tokens.shape[0]
    device_index = lax.axis_index("seq")
    query_pos = device_index * rows_here + jnp.arange(rows_here, dtype=jnp.int32)
    cosine, sine = rope_tables(query_pos - query_start)
    projected = jnp.dot(tokens, w_qkv, preferred_element_type=F32)
    merged_grad, out_term = middle(
        projected, cotangent[0], w_out, query_start.reshape(rows_here, 1), cosine, sine
    )
    input_grad = mm(merged_grad, w_qkv, NT).astype(BF16)[None]
    qkv_grad, out_rows = reduce_terms(tokens, merged_grad, out_term)
    return (input_grad, qkv_grad, out_rows.T)


def solution(mesh):
    return jax.shard_map(
        per_device,
        mesh=mesh,
        in_specs=(P("dp", "seq", None), P("dp", "seq", None), P(), P(), P("dp", "seq")),
        out_specs=(P("dp", "seq", None), P(("seq", "dp"), None), P(None, ("seq", "dp"))),
        check_vma=False,
    )
```

```python
import jax
import jax.numpy as jnp
from jax import lax
from jax.experimental import pallas as pl
from jax.experimental.pallas import tpu as pltpu
from jax.sharding import PartitionSpec as P

HEAD = 128
HEADS = 4
SPAN = 4


rope_theta = 500000.0


def rope_tables(offsets):
    half_width = HEAD // 2
    frequency = rope_theta ** (-2.0 * jnp.arange(half_width, dtype=jnp.float32) / HEAD)
    angles = offsets.astype(jnp.float32)[:, None] * frequency[None, :]
    cosine, sine = jnp.cos(angles), jnp.sin(angles)
    return (jnp.concatenate([cosine, cosine], axis=1), jnp.concatenate([-sine, sine], axis=1))


AXES = 4
ROWS = 32
LANES = 128
STREAMS = 10
Q_STREAMS = tuple(range(6))
O_STREAMS = tuple(range(6, 10))
CHUNKS = 4
BF16 = jnp.bfloat16
F32 = jnp.float32
MESH_ID = pl.DeviceIdType.MESH


def even_pair(i):
    return i + 1 - 2 * (i % 2)


def odd_pair(i):
    return (i + 3 - 2 * (i % 2)) % AXES


def stream_plan(g):
    order = ((0, 1, 2), (1, 2, 0), (2, 0, 1))[g % 3]
    first, second = (even_pair, odd_pair) if (g // 3) % 2 == 0 else (odd_pair, even_pair)
    return order, first, second


def device_of(x, y, z, core):
    return ((((y // 2) * AXES + z) * AXES + x) * 2 + core, y % 2)


def reduce_kernel(tok_ref, mg_ref, o_ref, q_out, o_out, q_ref, q_in, o_in, held, r1a, r1b, r2a, r2b, r3a, r3b, sib_sem, send_sem, recv_sem):
    seq = lax.axis_index("seq")
    dp = lax.axis_index("dp")
    core = seq % 2
    here = ((seq // 2) % AXES, (seq // 32) * 2 + dp, (seq // 8) % AXES)
    sibling = device_of(here[0], here[1], here[2], 1 - core)

    def moved(axis, value):
        spot = list(here)
        spot[axis] = value
        return device_of(*spot, core)

    barrier = pltpu.get_barrier_semaphore()
    pl.semaphore_signal(barrier, inc=1, device_id=sibling, device_id_type=MESH_ID)
    for axis in range(3):
        for pair in (even_pair, odd_pair):
            pl.semaphore_signal(barrier, inc=1, device_id=moved(axis, pair(here[axis])), device_id_type=MESH_ID)

    span = 2 * AXES * AXES // CHUNKS

    def multiply(chunk):
        def pair(k, _):
            at = chunk * span + 2 * k
            cols = pl.ds(pl.multiple_of(at * 4 * ROWS, 8 * ROWS), 8 * ROWS)
            term = mm(tok_ref[:, cols], mg_ref[...], TN).astype(BF16)
            q_ref[pl.ds(at, 2)] = term.reshape(2, 2, 2 * ROWS, 768)
            return 0

        lax.fori_loop(0, span // 2, pair, 0)

    def swap(n, src, dst):
        return pltpu.make_async_remote_copy(
            src_ref=src,
            dst_ref=dst,
            send_sem=sib_sem.at[0, n],
            recv_sem=sib_sem.at[1, n],
            device_id=sibling,
            device_id_type=MESH_ID,
        )

    def combine(own, got, streams, start, count):
        def step(k, _):
            block = start + k
            y_hi = block // 16
            z = (block // 4) % 4
            x = block % 4
            for y_lo in range(2):
                spot = (x, y_hi * 2 + y_lo, z)
                rows = slice(y_lo * ROWS, (y_lo + 1) * ROWS)
                for g in streams:
                    order, _, _ = stream_plan(g)
                    place = (spot[order[0]] * AXES + spot[order[1]]) * AXES + spot[order[2]]
                    col = g - streams[0]
                    cols = slice(col * LANES, (col + 1) * LANES)
                    total = own[block, core, rows, cols].astype(F32) + got[block, rows, cols].astype(F32)
                    held[g, place] = total.astype(BF16)
            return 0

        lax.fori_loop(0, count, step, 0)

    def copy(src, dst, g, n, target):
        return pltpu.make_async_remote_copy(
            src_ref=src,
            dst_ref=dst,
            send_sem=send_sem.at[g, n],
            recv_sem=recv_sem.at[g, n],
            device_id=target,
            device_id_type=MESH_ID,
        )

    def add_into(dst, dst_at, src, src_at):
        total = dst[dst_at].astype(F32) + src[src_at].astype(F32)
        dst[dst_at] = total.astype(BF16)

    bufs = ((r1a, r1b), (r2a, r2b), (r3a, r3b))
    sizes = (16, 4, 1)
    sends = {}

    def source(g, stage):
        if stage == 0:
            return held, g
        return bufs[stage - 1][1], g

    def start_first(g, stage):
        order, first, second = stream_plan(g)
        i = here[order[stage]]
        size = sizes[stage]
        f = first(i)
        src, _ = source(g, stage)
        for slot, index in ((1, second(f)), (0, f)):
            sends[g, stage, slot] = copy(
                src.at[g, pl.ds(index * size, size)],
                bufs[stage][0].at[g, slot],
                g,
                stage * 3 + slot,
                moved(order[stage], f),
            )
            sends[g, stage, slot].start()

    swaps = []
    for chunk in range(CHUNKS):
        multiply(chunk)
        if chunk == 0:
            pl.semaphore_wait(barrier, 7)
            swaps.append(swap(CHUNKS, o_ref.at[:, 1 - core], o_in))
            swaps[0].start()
        part = pl.ds(chunk * span, span)
        swaps.append(swap(chunk, q_ref.at[part, 1 - core], q_in.at[part]))
        swaps[-1].start()
        if chunk == 1:
            swaps[0].wait_recv()
            combine(o_ref, o_in, O_STREAMS, 0, 2 * AXES * AXES)
            for g in O_STREAMS:
                start_first(g, 0)
    for chunk in range(CHUNKS):
        swaps[1 + chunk].wait_recv()
        combine(q_ref, q_in, Q_STREAMS, chunk * span, span)
    for g in Q_STREAMS:
        start_first(g, 0)
    for stage in range(3):
        size = sizes[stage]
        for g in O_STREAMS + Q_STREAMS:
            order, first, second = stream_plan(g)
            i = here[order[stage]]
            s = second(i)
            src, _ = source(g, stage)
            sends[g, stage, 1].wait_recv()
            add_into(bufs[stage][0], (g, 1), src, (g, pl.ds(s * size, size)))
            sends[g, stage, 2] = copy(bufs[stage][0].at[g, 1], bufs[stage][1].at[g], g, stage * 3 + 2, moved(order[stage], s))
            sends[g, stage, 2].start()
            sends[g, stage, 0].wait_recv()
            add_into(bufs[stage][0], (g, 0), src, (g, pl.ds(i * size, size)))
        for g in O_STREAMS + Q_STREAMS:
            sends[g, stage, 2].wait_recv()
            if stage < 2:
                add_into(bufs[stage][1], (g,), bufs[stage][0], (g, 0))
                start_first(g, stage + 1)
            else:
                total = r3b[g, 0].astype(F32) + r3a[g, 0, 0].astype(F32)
                if g < 6:
                    q_out[:, g * LANES : (g + 1) * LANES] = total
                else:
                    o_out[:, (g - 6) * LANES : (g - 5) * LANES] = total
    for item in swaps:
        item.wait_send()
    for send in sends.values():
        send.wait_send()


def reduce_terms(tokens, merged_grad, o_term):
    vmem = pl.BlockSpec(memory_space=pltpu.VMEM)
    tile = (ROWS, LANES)
    return pl.pallas_call(
        reduce_kernel,
        out_shape=(
            jax.ShapeDtypeStruct((ROWS, 768), F32),
            jax.ShapeDtypeStruct((ROWS, 512), F32),
        ),
        in_specs=[vmem, vmem, vmem],
        out_specs=(vmem, vmem),
        scratch_shapes=[
            pltpu.VMEM((32, 2, 2 * ROWS, 768), BF16),
            pltpu.VMEM((32, 2 * ROWS, 768), BF16),
            pltpu.VMEM((32, 2 * ROWS, 512), BF16),
            pltpu.VMEM((STREAMS, 64) + tile, BF16),
            pltpu.VMEM((STREAMS, 2, 16) + tile, BF16),
            pltpu.VMEM((STREAMS, 16) + tile, BF16),
            pltpu.VMEM((STREAMS, 2, 4) + tile, BF16),
            pltpu.VMEM((STREAMS, 4) + tile, BF16),
            pltpu.VMEM((STREAMS, 2, 1) + tile, BF16),
            pltpu.VMEM((STREAMS, 1) + tile, BF16),
            pltpu.SemaphoreType.DMA((2, CHUNKS + 1)),
            pltpu.SemaphoreType.DMA((STREAMS, 9)),
            pltpu.SemaphoreType.DMA((STREAMS, 9)),
        ],
        compiler_params=pltpu.CompilerParams(
            collective_id=0, has_side_effects=True, vmem_limit_bytes=60 * 1024 * 1024
        ),
    )(tokens, merged_grad, o_term.reshape(32, 2, 2 * ROWS, 512))


NT = (((1,), (1,)), ((), ()))
NN = (((1,), (0,)), ((), ()))
TN = (((0,), (0,)), ((), ()))
LOG2E = 1.4426950408889634
TOK = 512
QROWS = 256
FAR = -1e30


def mm(a, b, dims):
    return lax.dot_general(a, b, dims, preferred_element_type=F32)


def middle_kernel(
    proj_ref, up_ref, w_ref, start_ref, cos_ref, sin_ref, merged_ref, term_ref,
    kv_ref, g_ref, att_ref, dkv_ref, far_ref, back_ref, send_sem, recv_sem,
):
    scale = HEAD**-0.5
    c = scale * LOG2E
    width = HEADS * HEAD
    seq = lax.axis_index("seq")
    dp_index = lax.axis_index("dp")
    count = lax.axis_size("seq")
    first = seq * TOK

    def peer(distance):
        return (lax.rem(seq + distance + count, count), dp_index)

    barrier = pltpu.get_barrier_semaphore()
    for d in range(1, SPAN):
        for distance in (d, -d):
            pl.semaphore_signal(barrier, inc=1, device_id=peer(distance), device_id_type=MESH_ID)

    def turn(v, rows):
        return v * cos_ref[rows, :] + pltpu.roll(v, HEAD // 2, 1) * sin_ref[rows, :]

    def turn_back(v, rows):
        return v * cos_ref[rows, :] + pltpu.roll(v * sin_ref[rows, :], HEAD // 2, 1)

    everything = slice(0, TOK)
    kv_ref[0, :, :HEAD] = turn(proj_ref[:, width : width + HEAD], everything).astype(BF16)
    kv_ref[0, :, HEAD:] = proj_ref[:, width + HEAD :].astype(BF16)
    dkv_ref[...] = jnp.zeros_like(dkv_ref)
    pl.semaphore_wait(barrier, 2 * (SPAN - 1))

    def copy(n, src, dst, distance):
        return pltpu.make_async_remote_copy(
            src_ref=src,
            dst_ref=dst,
            send_sem=send_sem.at[n],
            recv_sem=recv_sem.at[n],
            device_id=peer(distance),
            device_id_type=MESH_ID,
        )

    core = lax.rem(seq, 2)
    hop = copy(0, kv_ref.at[0], kv_ref.at[2], 2)
    near = copy(1, kv_ref.at[2], kv_ref.at[3 - 2 * core], 1 - 2 * core)
    onward = copy(2, kv_ref.at[2 * core], kv_ref.at[1 + 2 * core], 1)
    ahead = [hop, near, onward]
    hop.start()
    for block in range(TOK // QROWS):
        rows = slice(block * QROWS, (block + 1) * QROWS)
        g_ref[rows, :] = mm(up_ref[rows, :], w_ref[...], NT).astype(BF16)
        if block == 0:
            hop.wait_recv()
            near.start()
            onward.start()
    near.wait_recv()
    onward.wait_recv()

    def head(h, _):
        cols = pl.ds(pl.multiple_of(h * HEAD, HEAD), HEAD)
        for block in range(TOK // QROWS):
            rows = slice(block * QROWS, (block + 1) * QROWS)
            q = turn(proj_ref[rows, cols], rows).astype(BF16)
            g = g_ref[rows, cols]
            start = start_ref[rows, :]
            widths = [(block + 1) * QROWS] + [TOK] * (SPAN - 1)
            scores, bias = [], []
            top = None
            for d in range(SPAN):
                s = mm(q, kv_ref[d, : widths[d], :HEAD], NT)
                if d == 0:
                    col = lax.broadcasted_iota(jnp.int32, s.shape, 1)
                    row = lax.broadcasted_iota(jnp.int32, s.shape, 0) + block * QROWS
                    s = jnp.where((col <= row) & (col >= start - first), s, FAR)
                    b = 0.0
                    top = jnp.max(s, axis=1, keepdims=True)
                else:
                    b = jnp.where(start <= first - d * TOK, 0.0, FAR)
                    top = jnp.maximum(top, jnp.max(s, axis=1, keepdims=True) + b)
                scores.append(s)
                bias.append(b)
            top = top * c
            exps = [jnp.exp2(scores[d] * c + (bias[d] - top)) for d in range(SPAN)]
            inverse = 1.0 / sum(jnp.sum(e, axis=1, keepdims=True) for e in exps)
            probs = [e * inverse for e in exps]
            rounded = [p.astype(BF16) for p in probs]
            att = sum(mm(rounded[d], kv_ref[d, : widths[d], HEAD:], NN) for d in range(SPAN)).astype(BF16)
            att_ref[rows, cols] = att
            delta = jnp.sum(g.astype(F32) * att.astype(F32), axis=1, keepdims=True)
            dq = 0.0
            for d in range(SPAN):
                w = widths[d]
                dp = mm(g, kv_ref[d, :w, HEAD:], NT)
                ds = (probs[d] * (dp - delta)).astype(BF16)
                dq = dq + mm(ds, kv_ref[d, :w, :HEAD], NN)
                dkv_ref[d, :w, :HEAD] += mm(ds, q, TN)
                dkv_ref[d, :w, HEAD:] += mm(rounded[d], g, TN)
            merged_ref[rows, cols] = turn_back(dq * scale, rows).astype(BF16)
        return 0

    lax.fori_loop(0, HEADS, head, 0)
    for d in range(1, SPAN):
        far_ref[d - 1, :, :HEAD] = (dkv_ref[d, :, :HEAD] * scale).astype(BF16)
        far_ref[d - 1, :, HEAD:] = dkv_ref[d, :, HEAD:].astype(BF16)
    behind = [copy(SPAN - 2 + d, far_ref.at[d - 1], back_ref.at[d - 1], -d) for d in range(1, SPAN)]
    for item in behind:
        item.start()

    def term(i, _):
        cols = pl.ds(pl.multiple_of(i * TOK, TOK), TOK)
        term_ref[cols, :] = mm(up_ref[:, cols], att_ref[...], TN).astype(BF16)
        return 0

    lax.fori_loop(0, up_ref.shape[1] // TOK, term, 0)
    for item in behind:
        item.wait_recv()
    key = dkv_ref[0, :, :HEAD] * scale
    value = dkv_ref[0, :, HEAD:]
    for d in range(SPAN - 1):
        key = key + back_ref[d, :, :HEAD].astype(F32)
        value = value + back_ref[d, :, HEAD:].astype(F32)
    merged_ref[:, width : width + HEAD] = turn_back(key, everything).astype(BF16)
    merged_ref[:, width + HEAD :] = value.astype(BF16)
    for item in ahead + behind:
        item.wait_send()


def middle(projected, upstream, w_out, start, cosine, sine):
    vmem = pl.BlockSpec(memory_space=pltpu.VMEM)
    width = HEADS * HEAD
    return pl.pallas_call(
        middle_kernel,
        out_shape=(
            jax.ShapeDtypeStruct((TOK, width + 2 * HEAD), BF16),
            jax.ShapeDtypeStruct((upstream.shape[1], width), BF16),
        ),
        in_specs=[vmem] * 6,
        out_specs=(vmem, vmem),
        scratch_shapes=[
            pltpu.VMEM((SPAN, TOK, 2 * HEAD), BF16),
            pltpu.VMEM((TOK, width), BF16),
            pltpu.VMEM((TOK, width), BF16),
            pltpu.VMEM((SPAN, TOK, 2 * HEAD), F32),
            pltpu.VMEM((SPAN - 1, TOK, 2 * HEAD), BF16),
            pltpu.VMEM((SPAN - 1, TOK, 2 * HEAD), BF16),
            pltpu.SemaphoreType.DMA((2 * (SPAN - 1),)),
            pltpu.SemaphoreType.DMA((2 * (SPAN - 1),)),
        ],
        compiler_params=pltpu.CompilerParams(
            collective_id=1, has_side_effects=True, vmem_limit_bytes=60 * 1024 * 1024
        ),
    )(projected, upstream, w_out, start, cosine, sine)


def per_device(inputs, cotangent, w_qkv, w_out, doc_start):
    tokens = inputs[0]
    query_start = doc_start[0]
    rows_here = tokens.shape[0]
    device_index = lax.axis_index("seq")
    query_pos = device_index * rows_here + jnp.arange(rows_here, dtype=jnp.int32)
    cosine, sine = rope_tables(query_pos - query_start)
    projected = jnp.dot(tokens, w_qkv, preferred_element_type=F32)
    merged_grad, out_term = middle(
        projected, cotangent[0], w_out, query_start.reshape(rows_here, 1), cosine, sine
    )
    input_grad = mm(merged_grad, w_qkv, NT).astype(BF16)[None]
    qkv_grad, out_rows = reduce_terms(tokens, merged_grad, out_term)
    return (input_grad, qkv_grad, out_rows.T)


def solution(mesh):
    return jax.shard_map(
        per_device,
        mesh=mesh,
        in_specs=(P("dp", "seq", None), P("dp", "seq", None), P(), P(), P("dp", "seq")),
        out_specs=(P("dp", "seq", None), P(("seq", "dp"), None), P(None, ("seq", "dp"))),
        check_vma=False,
    )
```
